512 devices in a mesh: leaf: 128 (over y, z, core), rhs: 4 (over x).
Axes of the slice: x: 4, y: 8, z: 8, core: 2. Of those that a mesh axis runs over, the one named last changes fastest.
Arguments:
- obs_coef: float32 [128, 32768], P('rhs', 'leaf'), may hold values from -0.75 to 0.75
- obs_data: float32 [320, 32768], P('rhs', 'leaf'), may hold values from -6 to 6
- obs_target: int32 [32768], P('leaf'), may hold values from 0 to 511, as said below
- leaf_map: int32 [512], replicated, may hold values from 0 to 511, as said below
- leaf_parent: int32 [512], replicated, may hold values from 0 to 7
- leaf_inv: float32 [512, 128, 128], P('leaf'), may hold values from -0.5 to 1.5
- leaf_off: float32 [512, 128, 128], P('leaf'), may hold values from -0.0625 to 0.0625
- top_inv: float32 [8, 128, 128], replicated, may hold values from -0.5 to 1.5
- top_rhs: float32 [8, 320, 128], P(None, 'rhs'), may hold values from -6 to 6
Outputs:
- leaf_solution: float32 [512, 320, 128], P('leaf', 'rhs')
- top_solution: float32 [8, 320, 128], P(None, 'rhs')
The draws below stay inside these ranges and needn't reach their ends.
Inputs may be any that keep to these rules, and one draw needn't show every extreme that they name: A permutation: supernode i is stored at position leaf_map[i], which lies on index leaf_map[i] // 4 of leaf. `obs_target`: the rows held by one index of leaf name supernodes stored on any one index of leaf at most 4 times; in every draw one index of leaf is named exactly 4 times by the rows of every index.
All inputs are finite; a program needn't handle non-finite values.
Results may differ from the reference program's by a relative error of at most 0.0003.
Values sent between devices are 32-bit elements; how exact they have to be, the bound alone decides.
No kernel may reach another device: no remote copies, remote signals or barrier semaphores. Data moves between devices by JAX's collectives and lax.ppermute only.
A program may use at most 64 MiB of HBM per device.

```python
import math
import jax
import jax.numpy as jnp
from jax import lax

BLOCK = 128
DATES = 320
NTOP = 8
LEAF_DEV = 4
OBS_DEV = 256
NLEAF = 512
OBS = 32768
CAP = 4
N_LEAF = 128


def placement_draw(key):
    base_key = jax.random.fold_in(key, 7)
    key_map, key_hot, key_score, key_member, key_shuffle = jax.random.split(base_key, 5)
    devices = NLEAF // LEAF_DEV
    slots_all = devices * CAP
    leaf_map = jax.random.permutation(key_map, NLEAF).astype(jnp.int32)
    holder = jnp.argsort(leaf_map).astype(jnp.int32)
    hot_owner = jax.random.randint(key_hot, (), 0, devices, dtype=jnp.int32)
    slot_index = jnp.arange(slots_all, dtype=jnp.int32)
    slot_owner = slot_index // CAP
    scores = jax.random.randint(key_score, (devices, slots_all), 0, 2 ** 16, dtype=jnp.int32) * slots_all + slot_index[None, :]
    sort_keys = jnp.where(slot_owner[None, :] == hot_owner, 0, 2 ** 28) + scores
    taken = jnp.argsort(sort_keys, axis=1)[:, :OBS_DEV].astype(jnp.int32)
    dest_owner = taken // CAP
    dest_owner = jax.random.permutation(key_shuffle, dest_owner, axis=1, independent=True)
    member = jax.random.randint(key_member, (devices, OBS_DEV), 0, LEAF_DEV, dtype=jnp.int32)
    obs_target = holder[dest_owner * LEAF_DEV + member].reshape(-1).astype(jnp.int32)
    return (leaf_map, obs_target)


def draw_leaf_map(key, part):
    return placement_draw(key)[0]


def draw_obs_target(key, part):
    return placement_draw(key)[1]


def lower_blocks(key, count):
    key_diag, key_off = jax.random.split(key)
    row_index = jnp.arange(BLOCK)[:, None]
    col_index = jnp.arange(BLOCK)[None, :]
    below_diag = row_index > col_index
    on_diag = row_index == col_index
    diagonal = jnp.exp(jax.random.uniform(key_diag, (count, BLOCK, 1), jnp.float32, math.log(0.5), math.log(1.5)))
    off_diag = 0.08 * jnp.clip(jax.random.normal(key_off, (count, BLOCK, BLOCK), jnp.float32), -6.0, 6.0)
    return jnp.where(below_diag, off_diag, 0.0) + jnp.where(on_diag, diagonal, 0.0)


def draw_leaf_inv(key, part):
    return lower_blocks(jax.random.fold_in(key, 11), NLEAF)


def draw_top_inv(key, part):
    return lower_blocks(jax.random.fold_in(key, 13), NTOP)


def with_ends(values, key, smallest, top_value):
    spot = [jax.random.randint(jax.random.fold_in(key, axis), (), 0, length) for axis, length in enumerate(values.shape)]
    longest = values.shape.index(max(values.shape))
    neighbour = spot[:longest] + [(spot[longest] + 1) % values.shape[longest]] + spot[longest + 1:]
    return values.at[tuple(spot)].set(smallest).at[tuple(neighbour)].set(top_value)


def level_of(stream_key, extent, pieces, low, high):
    loudness = 1.0
    for axis_at, shards_of in pieces:
        heights = jax.random.uniform(jax.random.fold_in(jax.random.fold_in(stream_key, 6), axis_at), (shards_of,), jnp.float32, low / len(pieces), high / len(pieces))
        loudness = loudness * jnp.repeat(jnp.exp(heights), extent[axis_at] // shards_of).reshape((-1,) + (1,) * (len(extent) - 1 - axis_at))
    return loudness


def scatter_about(key, shape, deviation, reach, cuts=(), kind=jnp.bfloat16):
    entries = jax.random.normal(key, shape, jnp.float32) * deviation
    if len(cuts) > 0:
        entries = level_of(key, shape, cuts, -0.22, 0.18) * entries
    return jnp.clip(entries, min=-reach, max=reach).astype(kind)


def setup_inputs(seed: int = 0) -> dict:
    key_list = jax.random.split(jax.random.key(seed), 10)
    obs_coef = scatter_about(key_list[0], (BLOCK, OBS), 0.125, 0.75, ((0, 4), (1, 128)), jnp.float32)
    obs_data = scatter_about(key_list[1], (DATES, OBS), 1.0, 6.0, ((0, 4), (1, 128)), jnp.float32)
    obs_target = draw_obs_target(jax.random.fold_in(key_list[9], 71), 0)
    leaf_map = draw_leaf_map(jax.random.fold_in(key_list[9], 71), 0)
    leaf_parent = with_ends(jax.random.randint(key_list[4], (NLEAF,), 0, NTOP), jax.random.fold_in(key_list[4], 1), 0, NTOP - 1).astype(jnp.int32)
    leaf_inv = draw_leaf_inv(jax.random.fold_in(key_list[9], 71), 0)
    leaf_off = scatter_about(key_list[6], (NLEAF, BLOCK, BLOCK), (BLOCK * NLEAF // NTOP) ** -0.5, 0.0625, ((0, 128),), jnp.float32)
    top_inv = draw_top_inv(jax.random.fold_in(key_list[9], 71), 0)
    top_rhs = scatter_about(key_list[8], (NTOP, DATES, BLOCK), 1.0, 6.0, ((1, 4),), jnp.float32)
    return {"obs_coef": obs_coef, "obs_data": obs_data, "obs_target": obs_target, "leaf_map": leaf_map, "leaf_parent": leaf_parent, "leaf_inv": leaf_inv, "leaf_off": leaf_off, "top_inv": top_inv, "top_rhs": top_rhs}


def reference(obs_coef, obs_data, obs_target, leaf_map, leaf_parent, leaf_inv, leaf_off, top_inv, top_rhs):
    highest = lax.Precision.HIGHEST
    position = leaf_map[obs_target].astype(jnp.int32)
    owner_dev = (position // LEAF_DEV).astype(jnp.int32)
    member = (position % LEAF_DEV).astype(jnp.int32)
    row_order = jnp.argsort(owner_dev, stable=True).astype(jnp.int32)
    most_rows = N_LEAF * CAP
    counts = jnp.sum((owner_dev[None, :] == jnp.arange(N_LEAF, dtype=jnp.int32)[:, None]).astype(jnp.int32), axis=1).astype(jnp.int32)
    starts = (jnp.cumsum(counts) - counts).astype(jnp.int32)
    pad_data = jnp.concatenate([obs_data[:, row_order], jnp.zeros((DATES, most_rows), obs_data.dtype)], axis=1)
    pad_coef = jnp.concatenate([obs_coef[:, row_order], jnp.zeros((BLOCK, most_rows), obs_coef.dtype)], axis=1)
    pad_member = jnp.concatenate([member[row_order], jnp.full((most_rows,), -1, jnp.int32)])

    def assemble(device):
        start = starts[device]
        data_rows = lax.dynamic_slice_in_dim(pad_data, start, most_rows, 1)
        coef_rows = lax.dynamic_slice_in_dim(pad_coef, start, most_rows, 1)
        slot_rows = lax.dynamic_slice_in_dim(pad_member, start, most_rows, 0)
        live_rows = jnp.arange(most_rows, dtype=jnp.int32) < counts[device]
        chosen = (slot_rows[None, :] == jnp.arange(LEAF_DEV, dtype=jnp.int32)[:, None]) & live_rows[None, :]
        spread = data_rows[None, :, :] * chosen[:, None, :].astype(data_rows.dtype)
        return jnp.einsum('ltr,cr->ltc', spread, coef_rows, precision=highest)

    leaf_rhs = lax.map(assemble, jnp.arange(N_LEAF, dtype=jnp.int32)).reshape(NLEAF, DATES, BLOCK)
    leaf_y = jnp.einsum('ktc,kdc->ktd', leaf_rhs, leaf_inv, precision=highest)
    holder = jnp.argsort(leaf_map).astype(jnp.int32)
    parent_pos = leaf_parent[holder].astype(jnp.int32)
    update = jnp.einsum('ktd,kcd->ktc', leaf_y, leaf_off, precision=highest)
    top_sum = jax.ops.segment_sum(update, parent_pos, num_segments=NTOP)
    top_y = jnp.einsum('ptc,pdc->ptd', top_rhs - top_sum, top_inv, precision=highest)
    top_solution = jnp.einsum('ptd,pdc->ptc', top_y, top_inv, precision=highest)
    from_top = top_solution[parent_pos]
    lifted = jnp.einsum('ktc,kcd->ktd', from_top, leaf_off, precision=highest)
    leaf_solution = jnp.einsum('ktc,kcd->ktd', leaf_y - lifted, leaf_inv, precision=highest)
    return leaf_solution, top_solution
```

```python
import jax
import jax.numpy as jnp
from jax import lax
from jax.sharding import Mesh, PartitionSpec as P

HI = lax.Precision.HIGHEST


def body(
    obs_coef, obs_data, obs_target, leaf_map, leaf_parent, leaf_inv, leaf_off, top_inv, top_rhs
):
    chips = lax.axis_size("chip")
    cores = lax.axis_size("core")
    q = lax.axis_index("chip")
    c = lax.axis_index("core")
    local = leaf_inv.shape[0]
    width = leaf_inv.shape[1]
    tops = top_inv.shape[0]
    dates = obs_data.shape[0]
    rows = obs_target.shape[0]
    shard = obs_coef.shape[0]
    total = leaf_map.shape[0]
    cap = 4
    slots = cores * cap
    half = tops // cores
    pieces = tops * dates // (chips * cores)
    span = dates // pieces

    ids = jnp.arange(total, dtype=jnp.int32)
    pos = jnp.sum(jnp.where(obs_target[:, None] == ids[None, :], leaf_map[None, :], 0), axis=1)
    owner = pos // local
    member = pos % local
    r = jnp.arange(rows, dtype=jnp.int32)
    earlier = (owner[:, None] == owner[None, :]) & (r[:, None] > r[None, :])
    rank = jnp.sum(earlier.astype(jnp.int32), axis=1)
    code = ((owner % cores) * chips + owner // cores) * slots + c * cap + rank
    meta = jnp.stack([(member + 1).astype(jnp.float32), code.astype(jnp.float32)])
    pad = jnp.zeros((6, rows), jnp.float32)
    payload = jnp.concatenate([obs_data, obs_coef, meta, pad], axis=0)
    pair = lax.all_gather(payload, "core", axis=0, tiled=False)
    codes = pair[:, dates + shard + 1, :]
    slot_ids = (c * chips * slots + jnp.arange(chips * slots, dtype=jnp.int32)).astype(jnp.float32)
    onehot = (slot_ids[:, None, None] == codes[None, :, :]).astype(jnp.float32)
    placed = lax.dot_general(onehot, pair, (((1, 2), (0, 2)), ((), ())), precision=HI)
    placed = jnp.pad(placed, ((0, 0), (0, 128 - placed.shape[1]))).reshape(chips, slots, 128)
    recv = lax.all_to_all(placed, "chip", 0, 0).reshape(chips * slots, 128)
    coef_t = lax.all_gather(recv[:, dates : dates + shard].T, "rhs", axis=0, tiled=True)
    data_t = recv[:, :dates].T
    mark = recv[:, dates + shard]
    want = (jnp.arange(local, dtype=jnp.int32) + 1).astype(jnp.float32)
    chosen = (mark[None, :] == want[:, None]).astype(jnp.float32)
    spread = (data_t[None] * chosen[:, None, :]).reshape(local * dates, chips * slots)
    rhs = lax.dot_general(spread, coef_t, (((1,), (1,)), ((), ())), precision=HI)
    rhs = rhs.reshape(local, dates, width)
    comb = jnp.einsum("lcd,lde->lce", leaf_off, leaf_inv, precision=HI)
    update = jnp.einsum("lte,lce->ltc", rhs, comb, precision=HI)
    both = lax.all_gather(update, "core", axis=0, tiled=True)

    solved = jnp.einsum("ltc,ldc->ltd", rhs, leaf_inv, precision=HI)
    base = jnp.einsum("ltc,lcd->ltd", solved, leaf_inv, precision=HI)

    first = q * cores * local
    places = first + jnp.arange(cores * local, dtype=jnp.int32)
    held = leaf_map[None, :] == places[:, None]
    parent = jnp.sum(jnp.where(held, leaf_parent[None, :], 0), axis=1)
    mine = c * half + jnp.arange(half, dtype=jnp.int32)
    to_top = (parent[None, :] == mine[:, None]).astype(jnp.float32)
    contrib = jnp.sum(to_top[:, :, None, None] * both[None], axis=1)
    parts = contrib.reshape(half, pieces, span, width).transpose(0, 2, 1, 3)
    parts = parts.reshape(chips, pieces * width)
    got = lax.all_to_all(parts, "chip", 0, 0)
    piece = jnp.sum(got, axis=0).reshape(pieces, width)

    p = c * half + q // span
    tt = q % span
    gram = jnp.einsum("pdc,pde->pce", top_inv, top_inv, precision=HI)
    gram_p = lax.dynamic_index_in_dim(gram, p, 0, keepdims=False)
    own_rhs = lax.dynamic_slice(
        top_rhs.reshape(tops, pieces, span, width), (p, 0, tt, 0), (1, pieces, 1, width)
    ).reshape(pieces, width)
    sol = lax.dot_general(own_rhs - piece, gram_p, (((1,), (0,)), ((), ())), precision=HI)
    out = jnp.broadcast_to(sol.reshape(1, pieces * width), (chips, pieces * width))
    full = lax.all_to_all(out, "chip", 0, 0)
    full = lax.all_gather(full, "core", axis=0, tiled=True)
    top_solution = full.reshape(tops, span, pieces, width).transpose(0, 2, 1, 3)
    top_solution = top_solution.reshape(tops, dates, width)

    my_parent = lax.dynamic_slice_in_dim(parent, c * local, local, 0)
    pick = (my_parent[:, None] == jnp.arange(tops, dtype=jnp.int32)[None, :]).astype(jnp.float32)
    from_top = jnp.sum(pick[:, :, None, None] * top_solution[None], axis=1)
    leaf_solution = base - jnp.einsum("ltc,lcd->ltd", from_top, comb, precision=HI)
    return (leaf_solution, top_solution)


def solution(mesh):
    devices = mesh.devices
    split = Mesh(devices.reshape(devices.shape[0] // 2, 2, -1), ("chip", "core", "rhs"))
    leaf = ("chip", "core")
    return jax.shard_map(
        body,
        mesh=split,
        in_specs=(
            P("rhs", leaf),
            P("rhs", leaf),
            P(leaf),
            P(),
            P(),
            P(leaf, None, None),
            P(leaf, None, None),
            P(),
            P(None, "rhs", None),
        ),
        out_specs=(P(leaf, "rhs", None), P(None, "rhs", None)),
        check_vma=False,
    )
```

```python
import jax
import jax.numpy as jnp
from jax import lax
from jax.experimental import pallas as pl
from jax.experimental.pallas import tpu as pltpu
from jax.sharding import Mesh, PartitionSpec as P

HI = lax.Precision.HIGHEST
CAP = 4
LANES = 128
NT = (((1,), (1,)), ((), ()))
NN = (((1,), (0,)), ((), ()))


def split3(x):
    hi = x.astype(jnp.bfloat16)
    rest = x - hi.astype(jnp.float32)
    mid = rest.astype(jnp.bfloat16)
    low = (rest - mid.astype(jnp.float32)).astype(jnp.bfloat16)
    return hi, mid, low


def pack_kernel(core_ref, map_ref, target_ref, data_ref, coef_ref, out_ref, feat_ref, *, local):
    cores, rows = target_ref.shape
    total = map_ref.shape[1]
    dates = data_ref.shape[1]
    shard = coef_ref.shape[1]
    slots = cores * CAP
    n_slots = out_ref.shape[0]
    owners = total // local
    f32, bf16, i32 = jnp.float32, jnp.bfloat16, jnp.int32
    own = core_ref[0]
    where_to = map_ref[...]
    owner_of = where_to // local
    table = jnp.concatenate(
        [owner_of, where_to % local] + [jnp.zeros((1, total), i32)] * 6, axis=0
    ).astype(f32).astype(bf16)
    ids = lax.broadcasted_iota(i32, (total, rows), 0)
    owner_ids = lax.broadcasted_iota(i32, (owners, rows), 0)
    before = (
        lax.broadcasted_iota(i32, (rows, rows), 0) < lax.broadcasted_iota(i32, (rows, rows), 1)
    ).astype(f32).astype(bf16)
    feat_ref[...] = jnp.zeros(feat_ref.shape, f32)
    codes = []
    for s in range(cores):
        hit = (ids == target_ref[s : s + 1, :]).astype(f32).astype(bf16)
        found = lax.dot_general(table, hit, NN, preferred_element_type=f32)
        owner = found[0:1, :].astype(i32)
        same = (owner_ids == owner).astype(f32)
        count = lax.dot_general(same.astype(bf16), before, NN, preferred_element_type=f32)
        rank = jnp.sum(same * count, axis=0, keepdims=True).astype(i32)
        slot = (owner // cores) * slots + s * CAP + rank
        codes.append(jnp.where(owner % cores == own, slot, -1))
        cols = slice(s * rows, (s + 1) * rows)
        feat_ref[0:dates, cols] = data_ref[s]
        feat_ref[dates : dates + shard, cols] = coef_ref[s]
        feat_ref[dates + shard : dates + shard + 1, cols] = found[1:2, :] + 1.0
    code = jnp.concatenate(codes, axis=1)
    put = (lax.broadcasted_iota(i32, (n_slots, cores * rows), 0) == code).astype(f32).astype(bf16)
    acc = None
    for part in split3(feat_ref[...]):
        term = lax.dot_general(put, part, NT, preferred_element_type=f32)
        acc = term if acc is None else acc + term
    out_ref[...] = acc


def turn_kernel(recv_ref, turned_ref, share_ref, *, dates):
    turned = recv_ref[...].T
    turned_ref[...] = turned
    shard = share_ref.shape[1]
    for i in range(share_ref.shape[0]):
        share_ref[i] = turned[dates : dates + shard, :]


def forward_kernel(turned_ref, coef_ref, comb_ref, rhs_ref, update_ref, *, shard):
    local, dates, _ = rhs_ref.shape
    data = turned_ref[0:dates, :]
    mark = turned_ref[dates + shard : dates + shard + 1, :]
    coef = coef_ref[...]
    for k in range(local):
        picked = jnp.where(mark == float(k + 1), data, 0.0)
        rhs = lax.dot_general(picked, coef, NT, precision=HI, preferred_element_type=jnp.float32)
        rhs_ref[k] = rhs
        update_ref[k] = lax.dot_general(
            rhs, comb_ref[k], NT, precision=HI, preferred_element_type=jnp.float32
        )


def middle_kernel(got_ref, rhs_ref, gram_ref, out_ref):
    pieces, width = rhs_ref.shape
    chips = got_ref.shape[0] // pieces
    sums = [
        jnp.sum(got_ref[pl.ds(k, chips, stride=pieces), :], axis=0, keepdims=True)
        for k in range(pieces)
    ]
    left = rhs_ref[...] - jnp.concatenate(sums, axis=0)
    left = jnp.concatenate([left, jnp.zeros((8 - pieces % 8, width), jnp.float32)], axis=0)
    sol = lax.dot_general(
        left, gram_ref[...], NN, precision=HI, preferred_element_type=jnp.float32
    )
    for k in range(pieces):
        out_ref[pl.ds(k, chips, stride=pieces), :] = jnp.broadcast_to(
            sol[k : k + 1, :], (chips, width)
        )


def last_kernel(parent_ref, top_ref, base_ref, comb_ref, out_ref):
    for k in range(out_ref.shape[0]):
        lifted = lax.dot_general(
            top_ref[parent_ref[k]],
            comb_ref[k],
            NN,
            precision=HI,
            preferred_element_type=jnp.float32,
        )
        out_ref[k] = base_ref[k] - lifted


VM = pl.BlockSpec(memory_space=pltpu.VMEM)
SM = pl.BlockSpec(memory_space=pltpu.SMEM)


def arr(*shape):
    return pltpu.VMEM(shape, jnp.float32)


def vmem(*arrays):
    return [pltpu.with_memory_space_constraint(a, pltpu.VMEM) for a in arrays]


def body(
    obs_coef, obs_data, obs_target, leaf_map, leaf_parent, leaf_inv, leaf_off, top_inv, top_rhs
):
    chips = lax.axis_size("chip")
    cores = lax.axis_size("core")
    planes = lax.axis_size("rhs")
    q = lax.axis_index("chip")
    c = lax.axis_index("core")
    local = leaf_inv.shape[0]
    width = leaf_inv.shape[1]
    tops = top_inv.shape[0]
    dates = obs_data.shape[0]
    shard = obs_coef.shape[0]
    total = leaf_map.shape[0]
    slots = cores * CAP
    n_slots = chips * slots
    half = tops // cores
    pieces = half * dates // chips
    span = dates // pieces

    pair_target = lax.all_gather(obs_target, "core", axis=0)
    pair_data = lax.all_gather(obs_data, "core", axis=0)
    pair_coef = lax.all_gather(obs_coef, "core", axis=0)
    rows = cores * obs_target.shape[0]
    placed = pl.pallas_call(
        lambda *refs: pack_kernel(*refs, local=local),
        out_shape=arr(n_slots, LANES),
        in_specs=[SM, VM, VM, VM, VM],
        out_specs=VM,
        scratch_shapes=[pltpu.VMEM((LANES, rows), jnp.float32)],
        name="pack",
    )(c.reshape(1), *vmem(leaf_map.reshape(1, total), pair_target, pair_data, pair_coef))
    recv = lax.all_to_all(placed.reshape(chips, slots, LANES), "chip", 0, 0)
    turned, share = pl.pallas_call(
        lambda *refs: turn_kernel(*refs, dates=dates),
        out_shape=(arr(LANES, n_slots), arr(planes, shard, n_slots)),
        in_specs=[VM],
        out_specs=(VM, VM),
        name="turn",
    )(*vmem(recv.reshape(n_slots, LANES)))
    coef = lax.all_to_all(share, "rhs", 0, 0).reshape(planes * shard, n_slots)
    comb = jnp.einsum("lcd,lde->lce", leaf_off, leaf_inv, precision=HI)
    rhs, update = pl.pallas_call(
        lambda *refs: forward_kernel(*refs, shard=shard),
        out_shape=(arr(local, dates, width), arr(local, dates, width)),
        in_specs=[VM, VM, VM],
        out_specs=(VM, VM),
        name="forward",
    )(*vmem(turned, coef, comb))
    both = lax.all_gather(update, "core", axis=0, tiled=True)

    first = q * cores * local
    places = first + jnp.arange(cores * local, dtype=jnp.int32)
    held = leaf_map[None, :] == places[:, None]
    parent = jnp.sum(jnp.where(held, leaf_parent[None, :], 0), axis=1)
    mine = c * half + jnp.arange(half, dtype=jnp.int32)
    to_top = (parent[None, :] == mine[:, None]).astype(jnp.float32)
    contrib = jnp.sum(to_top[:, :, None, None] * both[None], axis=1)
    parts = contrib.reshape(chips, 1, pieces * width)
    got = lax.all_to_all(parts, "chip", 0, 0)

    p = c * half + q // span
    own_inv = lax.dynamic_index_in_dim(top_inv, p, 0, keepdims=False)
    gram = lax.dot_general(own_inv, own_inv, (((0,), (0,)), ((), ())), precision=HI)
    own_rhs = lax.dynamic_slice(top_rhs, (p, (q % span) * pieces, 0), (1, pieces, width))
    out = pl.pallas_call(
        middle_kernel,
        out_shape=arr(chips * pieces, width),
        in_specs=[VM, VM, VM],
        out_specs=VM,
        name="middle",
    )(*vmem(got.reshape(chips * pieces, width), own_rhs.reshape(pieces, width), gram))
    full = lax.all_to_all(out.reshape(chips, 1, pieces * width), "chip", 0, 0)
    full = lax.all_gather(full.reshape(half, dates, width), "core", axis=0, tiled=True)

    solved = jnp.einsum("ltc,ldc->ltd", rhs, leaf_inv, precision=HI)
    base = jnp.einsum("ltc,lcd->ltd", solved, leaf_inv, precision=HI)
    leaf_solution = pl.pallas_call(
        last_kernel,
        out_shape=jax.ShapeDtypeStruct((local, dates, width), jnp.float32),
        in_specs=[SM, VM, VM, VM],
        out_specs=VM,
        name="last",
    )(lax.dynamic_slice_in_dim(parent, c * local, local, 0), *vmem(full, base, comb))
    return (leaf_solution, full)


def solution(mesh):
    devices = mesh.devices
    split = Mesh(devices.reshape(devices.shape[0] // 2, 2, -1), ("chip", "core", "rhs"))
    leaf = ("chip", "core")
    return jax.shard_map(
        body,
        mesh=split,
        in_specs=(
            P("rhs", leaf),
            P("rhs", leaf),
            P(leaf),
            P(),
            P(),
            P(leaf, None, None),
            P(leaf, None, None),
            P(),
            P(None, "rhs", None),
        ),
        out_specs=(P(leaf, "rhs", None), P(None, "rhs", None)),
        check_vma=False,
    )
```

```python
import jax
import jax.numpy as jnp
from jax import lax
from jax.experimental import pallas as pl
from jax.experimental.pallas import tpu as pltpu
from jax.sharding import Mesh, PartitionSpec as P

HI = lax.Precision.HIGHEST
CAP = 4
LANES = 128
NT = (((1,), (1,)), ((), ()))
NN = (((1,), (0,)), ((), ()))
F32, BF16, I32 = jnp.float32, jnp.bfloat16, jnp.int32


def split2(x):
    high = x.astype(BF16)
    return high, (x - high.astype(F32)).astype(BF16)


def dot(a, b, dims):
    return lax.dot_general(a, b, dims, preferred_element_type=F32)


def join_kernel(
    map_hbm, target_hbm, data_hbm, coef_hbm, out_ref, map_ref, target_ref, sems, *, local, cores
):
    dates, rows = data_hbm.shape
    shard = coef_hbm.shape[0]
    total = map_hbm.shape[1]
    copies = [
        pltpu.make_async_copy(map_hbm, map_ref, sems.at[0]),
        pltpu.make_async_copy(target_hbm, target_ref, sems.at[1]),
        pltpu.make_async_copy(data_hbm, out_ref.at[pl.ds(0, dates)], sems.at[2]),
        pltpu.make_async_copy(coef_hbm, out_ref.at[pl.ds(dates, shard)], sems.at[3]),
    ]
    for copy in copies:
        copy.start()
    owners = total // local
    chips = owners // cores
    ids = lax.broadcasted_iota(I32, (total, rows), 0)
    owner_ids = lax.broadcasted_iota(I32, (owners, rows), 0)
    before = (
        lax.broadcasted_iota(I32, (rows, rows), 0) < lax.broadcasted_iota(I32, (rows, rows), 1)
    ).astype(F32).astype(BF16)
    copies[0].wait()
    copies[1].wait()
    where_to = map_ref[...]
    table = jnp.concatenate(
        [where_to // local, where_to % local] + [jnp.zeros((1, total), I32)] * 6, axis=0
    ).astype(F32).astype(BF16)
    hit = (ids == target_ref[...]).astype(F32).astype(BF16)
    found = dot(table, hit, NN)
    owner = found[0:1, :].astype(I32)
    same = (owner_ids == owner).astype(F32)
    rank = jnp.sum(same * dot(same.astype(BF16), before, NN), axis=0, keepdims=True)
    slot = (owner // cores) * (cores * CAP) + rank.astype(I32)
    code = (owner % cores) * (chips * cores * CAP) + slot + lax.axis_index("core") * CAP
    tail = out_ref.shape[0] - dates - shard
    out_ref[dates + shard :, :] = jnp.concatenate(
        [found[1:2, :] + 1.0, code.astype(F32), jnp.zeros((tail - 2, rows), F32)], axis=0
    )
    copies[2].wait()
    copies[3].wait()


def pack_kernel(pair_ref, out_ref, *, code_row):
    cores, height, rows = pair_ref.shape
    n_slots = out_ref.shape[0]
    code = jnp.concatenate([pair_ref[s, code_row : code_row + 1, :] for s in range(cores)], axis=1)
    code = code.astype(I32) - lax.axis_index("core") * n_slots
    put = (lax.broadcasted_iota(I32, (n_slots, cores * rows), 0) == code).astype(F32).astype(BF16)
    rest = jnp.zeros((LANES - height, cores * rows), F32)
    feat = jnp.concatenate([pair_ref[s] for s in range(cores)], axis=1)
    feat = jnp.concatenate([feat, rest], axis=0)
    both = dot(put, jnp.concatenate(split2(feat), axis=0), NT)
    out_ref[...] = both[:, :LANES] + both[:, LANES:]


def turn_kernel(recv_ref, turned_ref, share_ref, *, dates):
    turned = recv_ref[...].T
    turned_ref[...] = turned
    shard = share_ref.shape[1]
    for i in range(share_ref.shape[0]):
        share_ref[i] = turned[dates : dates + shard, :]


def forward_kernel(turned_ref, coef_ref, comb_ref, rhs_ref, update_ref, *, shard):
    local, dates, _ = rhs_ref.shape
    data = turned_ref[0:dates, :]
    mark = turned_ref[dates + shard : dates + shard + 1, :]
    coef_high, coef_low = split2(coef_ref[...])
    coef = jnp.concatenate([coef_high, coef_high, coef_low], axis=1)
    picked = jnp.concatenate(
        [jnp.where(mark == float(k + 1), data, 0.0) for k in range(local)], axis=0
    )
    high, low = split2(picked)
    rhs = dot(jnp.concatenate([high, low, high], axis=1), coef, NT)
    high, low = split2(rhs)
    rows = jnp.concatenate([high, low, high], axis=1)
    for k in range(local):
        part = slice(k * dates, (k + 1) * dates)
        rhs_ref[k] = rhs[part]
        update_ref[k] = dot(rows[part], comb_ref[k], NN)


def reduce_kernel(both_ref, parent_ref, out_ref):
    half, dates, width = out_ref.shape
    first = lax.axis_index("core") * half
    for p in range(half):
        acc = None
        for k in range(both_ref.shape[0]):
            term = jnp.where(parent_ref[k : k + 1, :] == first + p, both_ref[k], 0.0)
            acc = term if acc is None else acc + term
        out_ref[p] = acc


def middle_kernel(got_ref, rhs_ref, gram_ref, out_ref):
    pieces, width = rhs_ref.shape
    chips = got_ref.shape[0] // pieces
    sums = [
        jnp.sum(got_ref[pl.ds(k, chips, stride=pieces), :], axis=0, keepdims=True)
        for k in range(pieces)
    ]
    left = rhs_ref[...] - jnp.concatenate(sums, axis=0)
    left = jnp.concatenate([left, jnp.zeros((8 - pieces % 8, width), F32)], axis=0)
    high, low = split2(left)
    sol = dot(jnp.concatenate([high, low, high], axis=1), gram_ref[...], NN)
    for k in range(pieces):
        out_ref[pl.ds(k, chips, stride=pieces), :] = jnp.broadcast_to(
            sol[k : k + 1, :], (chips, width)
        )


def last_kernel(parent_ref, top_ref, base_ref, comb_ref, out_hbm, top_hbm, out_ref, sems):
    local = out_ref.shape[0]
    tops = top_ref.shape[0]
    copy_top = pltpu.make_async_copy(top_ref, top_hbm, sems.at[0])
    copy_top.start()
    copies = []
    for k in range(local):
        parent = parent_ref[k : k + 1, :]
        x = jnp.where(parent == 0, top_ref[0], 0.0)
        for p in range(1, tops):
            x = jnp.where(parent == p, top_ref[p], x)
        high, low = split2(x)
        lifted = dot(jnp.concatenate([high, low, high], axis=1), comb_ref[k], NN)
        out_ref[k] = base_ref[k] - lifted
        copies.append(pltpu.make_async_copy(out_ref.at[k], out_hbm.at[k], sems.at[1 + k]))
        copies[-1].start()
    copy_top.wait()
    for copy in copies:
        copy.wait()


VM = pl.BlockSpec(memory_space=pltpu.VMEM)
ANY = pl.BlockSpec(memory_space=pl.ANY)


def arr(*shape):
    return pltpu.VMEM(shape, F32)


def vmem(*arrays):
    return [pltpu.with_memory_space_constraint(a, pltpu.VMEM) for a in arrays]


def triple(m):
    high = lax.reduce_precision(m, 8, 7)
    low = (m - high).astype(BF16)
    high = high.astype(BF16)
    return jnp.concatenate([high, high, low], axis=-2)


def body(
    obs_coef, obs_data, obs_target, leaf_map, leaf_parent, leaf_inv, leaf_off, top_inv, top_rhs
):
    chips = lax.axis_size("chip")
    cores = lax.axis_size("core")
    planes = lax.axis_size("rhs")
    q = lax.axis_index("chip")
    c = lax.axis_index("core")
    local = leaf_inv.shape[0]
    width = leaf_inv.shape[1]
    tops = top_inv.shape[0]
    dates, rows = obs_data.shape
    shard = obs_coef.shape[0]
    total = leaf_map.shape[0]
    slots = cores * CAP
    n_slots = chips * slots
    half = tops // cores
    pieces = half * dates // chips
    span = dates // pieces
    height = dates + shard + 8

    payload = pl.pallas_call(
        lambda *refs: join_kernel(*refs, local=local, cores=cores),
        out_shape=arr(height, rows),
        in_specs=[ANY, ANY, ANY, ANY],
        out_specs=VM,
        scratch_shapes=[
            pltpu.VMEM((1, total), I32),
            pltpu.VMEM((1, rows), I32),
            pltpu.SemaphoreType.DMA((4,)),
        ],
        name="join",
    )(leaf_map.reshape(1, total), obs_target.reshape(1, rows), obs_data, obs_coef)
    pair = lax.all_gather(payload, "core", axis=0)
    placed = pl.pallas_call(
        lambda *refs: pack_kernel(*refs, code_row=dates + shard + 1),
        out_shape=arr(n_slots, LANES),
        in_specs=[VM],
        out_specs=VM,
        name="pack",
    )(*vmem(pair))
    recv = lax.all_to_all(placed.reshape(chips, slots, LANES), "chip", 0, 0)
    turned, share = pl.pallas_call(
        lambda *refs: turn_kernel(*refs, dates=dates),
        out_shape=(arr(LANES, n_slots), arr(planes, shard, n_slots)),
        in_specs=[VM],
        out_specs=(VM, VM),
        name="turn",
    )(*vmem(recv.reshape(n_slots, LANES)))
    coef = lax.all_to_all(share, "rhs", 0, 0).reshape(planes * shard, n_slots)

    comb = jnp.einsum("lcd,lde->lce", leaf_off, leaf_inv, precision=HI)
    comb_t = jnp.einsum("lcd,lde->lec", leaf_off, leaf_inv, precision=HI)
    rhs, update = pl.pallas_call(
        lambda *refs: forward_kernel(*refs, shard=shard),
        out_shape=(arr(local, dates, width), arr(local, dates, width)),
        in_specs=[VM, VM, VM],
        out_specs=(VM, VM),
        name="forward",
    )(*vmem(turned, coef, triple(comb_t)))
    both = lax.all_gather(update, "core", axis=0, tiled=True)

    places = q * (cores * local) + jnp.arange(cores * local, dtype=I32)
    held = leaf_map[None, :] == places[:, None]
    parent = jnp.sum(jnp.where(held, leaf_parent[None, :], 0), axis=1)
    parent = jnp.broadcast_to(parent[:, None], (cores * local, LANES))
    contrib = pl.pallas_call(
        reduce_kernel,
        out_shape=arr(half, dates, width),
        in_specs=[VM, VM],
        out_specs=VM,
        name="reduce",
    )(*vmem(both, parent))
    got = lax.all_to_all(contrib.reshape(chips, 1, pieces * width), "chip", 0, 0)

    p = c * half + q // span
    own_inv = lax.dynamic_index_in_dim(top_inv, p, 0, keepdims=False)
    gram = lax.dot_general(own_inv, own_inv, (((0,), (0,)), ((), ())), precision=HI)
    own_rhs = lax.dynamic_slice(top_rhs, (p, (q % span) * pieces, 0), (1, pieces, width))
    out = pl.pallas_call(
        middle_kernel,
        out_shape=arr(chips * pieces, width),
        in_specs=[VM, VM, VM],
        out_specs=VM,
        name="middle",
    )(*vmem(got.reshape(chips * pieces, width), own_rhs.reshape(pieces, width), triple(gram)))
    full = lax.all_to_all(out.reshape(chips, 1, pieces * width), "chip", 0, 0)
    full = lax.all_gather(full.reshape(half, dates, width), "core", axis=0, tiled=True)

    solved = jnp.einsum("ltc,ldc->ltd", rhs, leaf_inv, precision=HI)
    base = jnp.einsum("ltc,lcd->ltd", solved, leaf_inv, precision=HI)
    own_parent = lax.dynamic_slice_in_dim(parent, c * local, local, 0)
    return pl.pallas_call(
        last_kernel,
        out_shape=(
            jax.ShapeDtypeStruct((local, dates, width), F32),
            jax.ShapeDtypeStruct((tops, dates, width), F32),
        ),
        in_specs=[VM, VM, VM, VM],
        out_specs=(ANY, ANY),
        scratch_shapes=[
            pltpu.VMEM((local, dates, width), F32),
            pltpu.SemaphoreType.DMA((1 + local,)),
        ],
        name="last",
    )(*vmem(own_parent, full, base, triple(comb)))


def solution(mesh):
    devices = mesh.devices
    split = Mesh(devices.reshape(devices.shape[0] // 2, 2, -1), ("chip", "core", "rhs"))
    leaf = ("chip", "core")
    return jax.shard_map(
        body,
        mesh=split,
        in_specs=(
            P("rhs", leaf),
            P("rhs", leaf),
            P(leaf),
            P(),
            P(),
            P(leaf, None, None),
            P(leaf, None, None),
            P(),
            P(None, "rhs", None),
        ),
        out_specs=(P(leaf, "rhs", None), P(None, "rhs", None)),
        check_vma=False,
    )
```

```python
import math

import jax
import jax.numpy as jnp
from jax import lax
from jax.experimental import pallas as pl
from jax.experimental.pallas import tpu as pltpu
from jax.sharding import Mesh, PartitionSpec as P

HI = lax.Precision.HIGHEST
CAP = 4
LANES = 128
NT = (((1,), (1,)), ((), ()))
NN = (((1,), (0,)), ((), ()))
F32, BF16, I32 = jnp.float32, jnp.bfloat16, jnp.int32


def far_index(count):
    side = math.isqrt(count)
    return side // 2 * side + side // 2


def exchange(x, axis, far):
    order = [i ^ far for i in range(x.shape[0])]
    return lax.all_to_all(x, axis, 0, 0, axis_index_groups=[order])


def split2(x):
    high = x.astype(BF16)
    return high, (x - high.astype(F32)).astype(BF16)


def dot(a, b, dims):
    return lax.dot_general(a, b, dims, preferred_element_type=F32)


def join_kernel(
    map_hbm, target_hbm, data_hbm, coef_hbm, out_ref, map_ref, target_ref, sems, *, local, cores
):
    dates, rows = data_hbm.shape
    shard = coef_hbm.shape[0]
    total = map_hbm.shape[1]
    copies = [
        pltpu.make_async_copy(map_hbm, map_ref, sems.at[0]),
        pltpu.make_async_copy(target_hbm, target_ref, sems.at[1]),
        pltpu.make_async_copy(data_hbm, out_ref.at[pl.ds(0, dates)], sems.at[2]),
        pltpu.make_async_copy(coef_hbm, out_ref.at[pl.ds(dates, shard)], sems.at[3]),
    ]
    for copy in copies:
        copy.start()
    owners = total // local
    chips = owners // cores
    ids = lax.broadcasted_iota(I32, (total, rows), 0)
    owner_ids = lax.broadcasted_iota(I32, (owners, rows), 0)
    before = (
        lax.broadcasted_iota(I32, (rows, rows), 0) < lax.broadcasted_iota(I32, (rows, rows), 1)
    ).astype(F32).astype(BF16)
    copies[0].wait()
    copies[1].wait()
    where_to = map_ref[...]
    table = jnp.concatenate(
        [where_to // local, where_to % local] + [jnp.zeros((1, total), I32)] * 6, axis=0
    ).astype(F32).astype(BF16)
    hit = (ids == target_ref[...]).astype(F32).astype(BF16)
    found = dot(table, hit, NN)
    owner = found[0:1, :].astype(I32)
    same = (owner_ids == owner).astype(F32)
    rank = jnp.sum(same * dot(same.astype(BF16), before, NN), axis=0, keepdims=True)
    slot = ((owner // cores) ^ far_index(chips)) * (cores * CAP) + rank.astype(I32)
    code = (owner % cores) * (chips * cores * CAP) + slot + lax.axis_index("core") * CAP
    tail = out_ref.shape[0] - dates - shard
    out_ref[dates + shard :, :] = jnp.concatenate(
        [found[1:2, :] + 1.0, code.astype(F32), jnp.zeros((tail - 2, rows), F32)], axis=0
    )
    copies[2].wait()
    copies[3].wait()


def pack_kernel(pair_ref, out_ref, *, code_row):
    cores, height, rows = pair_ref.shape
    n_slots = out_ref.shape[0]
    code = jnp.concatenate([pair_ref[s, code_row : code_row + 1, :] for s in range(cores)], axis=1)
    code = code.astype(I32) - lax.axis_index("core") * n_slots
    put = (lax.broadcasted_iota(I32, (n_slots, cores * rows), 0) == code).astype(F32).astype(BF16)
    rest = jnp.zeros((LANES - height, cores * rows), F32)
    feat = jnp.concatenate([pair_ref[s] for s in range(cores)], axis=1)
    feat = jnp.concatenate([feat, rest], axis=0)
    both = dot(put, jnp.concatenate(split2(feat), axis=0), NT)
    out_ref[...] = both[:, :LANES] + both[:, LANES:]


def turn_kernel(recv_ref, turned_ref, share_ref, *, dates):
    turned = recv_ref[...].T
    turned_ref[...] = turned
    shard = share_ref.shape[1]
    for i in range(share_ref.shape[0]):
        share_ref[i] = turned[dates : dates + shard, :]


def forward_kernel(turned_ref, coef_ref, comb_ref, rhs_ref, update_ref, *, shard):
    local, dates, _ = rhs_ref.shape
    data = turned_ref[0:dates, :]
    mark = turned_ref[dates + shard : dates + shard + 1, :]
    planes = coef_ref.shape[0]
    order = [coef_ref[i ^ (planes // 2)] for i in range(planes)]
    coef_high, coef_low = split2(jnp.concatenate(order, axis=0))
    coef = jnp.concatenate([coef_high, coef_high, coef_low], axis=1)
    picked = jnp.concatenate(
        [jnp.where(mark == float(k + 1), data, 0.0) for k in range(local)], axis=0
    )
    high, low = split2(picked)
    rhs = dot(jnp.concatenate([high, low, high], axis=1), coef, NT)
    high, low = split2(rhs)
    rows = jnp.concatenate([high, low, high], axis=1)
    for k in range(local):
        part = slice(k * dates, (k + 1) * dates)
        rhs_ref[k] = rhs[part]
        update_ref[k] = dot(rows[part], comb_ref[k], NN)


def reduce_kernel(both_ref, parent_ref, out_ref):
    half, dates, width = out_ref.shape
    first = lax.axis_index("core") * half
    for p in range(half):
        acc = None
        for k in range(both_ref.shape[0]):
            term = jnp.where(parent_ref[k : k + 1, :] == first + p, both_ref[k], 0.0)
            acc = term if acc is None else acc + term
        out_ref[p] = acc


def middle_kernel(got_ref, rhs_ref, gram_ref, out_ref):
    pieces, width = rhs_ref.shape
    chips = got_ref.shape[0] // pieces
    sums = [
        jnp.sum(got_ref[pl.ds(k, chips, stride=pieces), :], axis=0, keepdims=True)
        for k in range(pieces)
    ]
    left = rhs_ref[...] - jnp.concatenate(sums, axis=0)
    left = jnp.concatenate([left, jnp.zeros((8 - pieces % 8, width), F32)], axis=0)
    high, low = split2(left)
    sol = dot(jnp.concatenate([high, low, high], axis=1), gram_ref[...], NN)
    for k in range(pieces):
        out_ref[pl.ds(k, chips, stride=pieces), :] = jnp.broadcast_to(
            sol[k : k + 1, :], (chips, width)
        )


def last_kernel(parent_ref, top_ref, base_ref, comb_ref, out_hbm, top_hbm, out_ref, sems):
    local = out_ref.shape[0]
    tops = top_ref.shape[0]
    copy_top = pltpu.make_async_copy(top_ref, top_hbm, sems.at[0])
    copy_top.start()
    copies = []
    for k in range(local):
        parent = parent_ref[k : k + 1, :]
        x = jnp.where(parent == 0, top_ref[0], 0.0)
        for p in range(1, tops):
            x = jnp.where(parent == p, top_ref[p], x)
        high, low = split2(x)
        lifted = dot(jnp.concatenate([high, low, high], axis=1), comb_ref[k], NN)
        out_ref[k] = base_ref[k] - lifted
        copies.append(pltpu.make_async_copy(out_ref.at[k], out_hbm.at[k], sems.at[1 + k]))
        copies[-1].start()
    copy_top.wait()
    for copy in copies:
        copy.wait()


VM = pl.BlockSpec(memory_space=pltpu.VMEM)
ANY = pl.BlockSpec(memory_space=pl.ANY)


def arr(*shape):
    return pltpu.VMEM(shape, F32)


def vmem(*arrays):
    return [pltpu.with_memory_space_constraint(a, pltpu.VMEM) for a in arrays]


def triple(m):
    high = lax.reduce_precision(m, 8, 7)
    low = (m - high).astype(BF16)
    high = high.astype(BF16)
    return jnp.concatenate([high, high, low], axis=-2)


def body(
    obs_coef, obs_data, obs_target, leaf_map, leaf_parent, leaf_inv, leaf_off, top_inv, top_rhs
):
    chips = lax.axis_size("chip")
    cores = lax.axis_size("core")
    planes = lax.axis_size("rhs")
    q = lax.axis_index("chip")
    c = lax.axis_index("core")
    local = leaf_inv.shape[0]
    width = leaf_inv.shape[1]
    tops = top_inv.shape[0]
    dates, rows = obs_data.shape
    shard = obs_coef.shape[0]
    total = leaf_map.shape[0]
    slots = cores * CAP
    n_slots = chips * slots
    half = tops // cores
    pieces = half * dates // chips
    span = dates // pieces
    height = dates + shard + 8
    far = far_index(chips)

    payload = pl.pallas_call(
        lambda *refs: join_kernel(*refs, local=local, cores=cores),
        out_shape=arr(height, rows),
        in_specs=[ANY, ANY, ANY, ANY],
        out_specs=VM,
        scratch_shapes=[
            pltpu.VMEM((1, total), I32),
            pltpu.VMEM((1, rows), I32),
            pltpu.SemaphoreType.DMA((4,)),
        ],
        name="join",
    )(leaf_map.reshape(1, total), obs_target.reshape(1, rows), obs_data, obs_coef)
    pair = lax.all_gather(payload, "core", axis=0)
    placed = pl.pallas_call(
        lambda *refs: pack_kernel(*refs, code_row=dates + shard + 1),
        out_shape=arr(n_slots, LANES),
        in_specs=[VM],
        out_specs=VM,
        name="pack",
    )(*vmem(pair))
    recv = exchange(placed.reshape(chips, slots, LANES), "chip", far)
    turned, share = pl.pallas_call(
        lambda *refs: turn_kernel(*refs, dates=dates),
        out_shape=(arr(LANES, n_slots), arr(planes, shard, n_slots)),
        in_specs=[VM],
        out_specs=(VM, VM),
        name="turn",
    )(*vmem(recv.reshape(n_slots, LANES)))
    coef = exchange(share, "rhs", planes // 2)

    comb = jnp.einsum("lcd,lde->lce", leaf_off, leaf_inv, precision=HI)
    comb_t = jnp.einsum("lcd,lde->lec", leaf_off, leaf_inv, precision=HI)
    rhs, update = pl.pallas_call(
        lambda *refs: forward_kernel(*refs, shard=shard),
        out_shape=(arr(local, dates, width), arr(local, dates, width)),
        in_specs=[VM, VM, VM],
        out_specs=(VM, VM),
        name="forward",
    )(*vmem(turned, coef, triple(comb_t)))
    both = lax.all_gather(update, "core", axis=0, tiled=True)

    places = q * (cores * local) + jnp.arange(cores * local, dtype=I32)
    held = leaf_map[None, :] == places[:, None]
    parent = jnp.sum(jnp.where(held, leaf_parent[None, :], 0), axis=1)
    parent = jnp.broadcast_to(parent[:, None], (cores * local, LANES))
    contrib = pl.pallas_call(
        reduce_kernel,
        out_shape=arr(half, dates, width),
        in_specs=[VM, VM],
        out_specs=VM,
        name="reduce",
    )(*vmem(both, parent))
    got = exchange(contrib.reshape(chips, 1, pieces * width), "chip", far)

    piece = q ^ far
    p = c * half + piece // span
    own_inv = lax.dynamic_index_in_dim(top_inv, p, 0, keepdims=False)
    gram = lax.dot_general(own_inv, own_inv, (((0,), (0,)), ((), ())), precision=HI)
    own_rhs = lax.dynamic_slice(top_rhs, (p, (piece % span) * pieces, 0), (1, pieces, width))
    out = pl.pallas_call(
        middle_kernel,
        out_shape=arr(chips * pieces, width),
        in_specs=[VM, VM, VM],
        out_specs=VM,
        name="middle",
    )(*vmem(got.reshape(chips * pieces, width), own_rhs.reshape(pieces, width), triple(gram)))
    full = exchange(out.reshape(chips, 1, pieces * width), "chip", far)
    full = lax.all_gather(full.reshape(half, dates, width), "core", axis=0, tiled=True)

    solved = jnp.einsum("ltc,ldc->ltd", rhs, leaf_inv, precision=HI)
    base = jnp.einsum("ltc,lcd->ltd", solved, leaf_inv, precision=HI)
    own_parent = lax.dynamic_slice_in_dim(parent, c * local, local, 0)
    return pl.pallas_call(
        last_kernel,
        out_shape=(
            jax.ShapeDtypeStruct((local, dates, width), F32),
            jax.ShapeDtypeStruct((tops, dates, width), F32),
        ),
        in_specs=[VM, VM, VM, VM],
        out_specs=(ANY, ANY),
        scratch_shapes=[
            pltpu.VMEM((local, dates, width), F32),
            pltpu.SemaphoreType.DMA((1 + local,)),
        ],
        name="last",
    )(*vmem(own_parent, full, base, triple(comb)))


def solution(mesh):
    devices = mesh.devices
    split = Mesh(devices.reshape(devices.shape[0] // 2, 2, -1), ("chip", "core", "rhs"))
    leaf = ("chip", "core")
    return jax.shard_map(
        body,
        mesh=split,
        in_specs=(
            P("rhs", leaf),
            P("rhs", leaf),
            P(leaf),
            P(),
            P(),
            P(leaf, None, None),
            P(leaf, None, None),
            P(),
            P(None, "rhs", None),
        ),
        out_specs=(P(leaf, "rhs", None), P(None, "rhs", None)),
        check_vma=False,
    )
```

```python
import math

import jax
import jax.numpy as jnp
from jax import lax
from jax.experimental import pallas as pl
from jax.experimental.pallas import tpu as pltpu
from jax.sharding import Mesh, PartitionSpec as P

HI = lax.Precision.HIGHEST
CAP = 4
LANES = 128
NT = (((1,), (1,)), ((), ()))
NN = (((1,), (0,)), ((), ()))
F32, BF16, I32 = jnp.float32, jnp.bfloat16, jnp.int32


def far_index(count):
    side = math.isqrt(count)
    return side // 2 * side + side // 2


def exchange(x, axis, far):
    order = [i ^ far for i in range(x.shape[0])]
    return lax.all_to_all(x, axis, 0, 0, axis_index_groups=[order])


def split2(x):
    high = x.astype(BF16)
    return high, (x - high.astype(F32)).astype(BF16)


def dot(a, b, dims):
    return lax.dot_general(a, b, dims, preferred_element_type=F32)


def join_kernel(
    map_hbm, target_hbm, data_hbm, coef_hbm, out_ref, map_ref, target_ref, sems, *, local, cores
):
    dates, rows = data_hbm.shape
    shard = coef_hbm.shape[0]
    total = map_hbm.shape[1]
    copies = [
        pltpu.make_async_copy(map_hbm, map_ref, sems.at[0]),
        pltpu.make_async_copy(target_hbm, target_ref, sems.at[1]),
        pltpu.make_async_copy(data_hbm, out_ref.at[pl.ds(0, dates)], sems.at[2]),
        pltpu.make_async_copy(coef_hbm, out_ref.at[pl.ds(dates, shard)], sems.at[3]),
    ]
    for copy in copies:
        copy.start()
    owners = total // local
    chips = owners // cores
    ids = lax.broadcasted_iota(I32, (total, rows), 0)
    owner_ids = lax.broadcasted_iota(I32, (owners, rows), 0)
    before = (
        lax.broadcasted_iota(I32, (rows, rows), 0) < lax.broadcasted_iota(I32, (rows, rows), 1)
    ).astype(F32).astype(BF16)
    copies[0].wait()
    copies[1].wait()
    where_to = map_ref[...]
    table = jnp.concatenate(
        [where_to // local, where_to % local] + [jnp.zeros((1, total), I32)] * 6, axis=0
    ).astype(F32).astype(BF16)
    hit = (ids == target_ref[...]).astype(F32).astype(BF16)
    found = dot(table, hit, NN)
    owner = found[0:1, :].astype(I32)
    same = (owner_ids == owner).astype(F32)
    rank = jnp.sum(same * dot(same.astype(BF16), before, NN), axis=0, keepdims=True)
    slot = ((owner // cores) ^ far_index(chips)) * (cores * CAP) + rank.astype(I32)
    code = (owner % cores) * (chips * cores * CAP) + slot + lax.axis_index("core") * CAP
    tail = out_ref.shape[0] - dates - shard
    out_ref[dates + shard :, :] = jnp.concatenate(
        [found[1:2, :] + 1.0, code.astype(F32), jnp.zeros((tail - 2, rows), F32)], axis=0
    )
    copies[2].wait()
    copies[3].wait()


def pack_kernel(pair_ref, out_ref, *, code_row):
    cores, height, rows = pair_ref.shape
    n_slots = out_ref.shape[0]
    code = jnp.concatenate([pair_ref[s, code_row : code_row + 1, :] for s in range(cores)], axis=1)
    code = code.astype(I32) - lax.axis_index("core") * n_slots
    put = (lax.broadcasted_iota(I32, (n_slots, cores * rows), 0) == code).astype(F32).astype(BF16)
    rest = jnp.zeros((LANES - height, cores * rows), F32)
    feat = jnp.concatenate([pair_ref[s] for s in range(cores)], axis=1)
    feat = jnp.concatenate([feat, rest], axis=0)
    both = dot(put, jnp.concatenate(split2(feat), axis=0), NT)
    out_ref[...] = both[:, :LANES] + both[:, LANES:]


def turn_kernel(recv_ref, turned_ref, share_ref, *, dates):
    turned = recv_ref[...].T
    turned_ref[...] = turned
    shard = share_ref.shape[1]
    for i in range(share_ref.shape[0]):
        share_ref[i] = turned[dates : dates + shard, :]


def forward_kernel(turned_ref, coef_ref, comb_ref, rows_ref, update_ref, *, shard):
    local, dates, _ = update_ref.shape
    data = turned_ref[0:dates, :]
    mark = turned_ref[dates + shard : dates + shard + 1, :]
    planes = coef_ref.shape[0]
    order = [coef_ref[i ^ (planes // 2)] for i in range(planes)]
    coef_high, coef_low = split2(jnp.concatenate(order, axis=0))
    coef = jnp.concatenate([coef_high, coef_high, coef_low], axis=1)
    picked = jnp.concatenate(
        [jnp.where(mark == float(k + 1), data, 0.0) for k in range(local)], axis=0
    )
    high, low = split2(picked)
    rhs = dot(jnp.concatenate([high, low, high], axis=1), coef, NT)
    high, low = split2(rhs)
    rows = jnp.concatenate([high, low, high], axis=1)
    rows_ref[...] = rows
    for k in range(local):
        update_ref[k] = dot(rows[k * dates : (k + 1) * dates], comb_ref[k], NN)


def reduce_kernel(both_ref, parent_ref, out_ref):
    half, dates, width = out_ref.shape
    first = lax.axis_index("core") * half
    for p in range(half):
        acc = None
        for k in range(both_ref.shape[0]):
            term = jnp.where(parent_ref[k : k + 1, :] == first + p, both_ref[k], 0.0)
            acc = term if acc is None else acc + term
        out_ref[p] = acc


def middle_kernel(got_ref, rhs_ref, gram_ref, out_ref):
    pieces, width = rhs_ref.shape
    chips = got_ref.shape[0] // pieces
    sums = [
        jnp.sum(got_ref[pl.ds(k, chips, stride=pieces), :], axis=0, keepdims=True)
        for k in range(pieces)
    ]
    left = rhs_ref[...] - jnp.concatenate(sums, axis=0)
    left = jnp.concatenate([left, jnp.zeros((8 - pieces % 8, width), F32)], axis=0)
    high, low = split2(left)
    sol = dot(jnp.concatenate([high, low, high], axis=1), gram_ref[...], NN)
    for k in range(pieces):
        out_ref[pl.ds(k, chips, stride=pieces), :] = jnp.broadcast_to(
            sol[k : k + 1, :], (chips, width)
        )


def last_kernel(parent_ref, top_ref, rows_ref, both_ref, out_hbm, top_hbm, out_ref, sems):
    local, dates, _ = out_ref.shape
    tops = top_ref.shape[0]
    copy_top = pltpu.make_async_copy(top_ref, top_hbm, sems.at[0])
    copy_top.start()
    copies = []
    for k in range(local):
        parent = parent_ref[k : k + 1, :]
        x = jnp.where(parent == 0, top_ref[0], 0.0)
        for p in range(1, tops):
            x = jnp.where(parent == p, top_ref[p], x)
        high, low = split2(x)
        rows = rows_ref[k * dates : (k + 1) * dates, :]
        out_ref[k] = dot(jnp.concatenate([rows, high, low, high], axis=1), both_ref[k], NN)
        copies.append(pltpu.make_async_copy(out_ref.at[k], out_hbm.at[k], sems.at[1 + k]))
        copies[-1].start()
    copy_top.wait()
    for copy in copies:
        copy.wait()


VM = pl.BlockSpec(memory_space=pltpu.VMEM)
ANY = pl.BlockSpec(memory_space=pl.ANY)


def arr(*shape):
    return pltpu.VMEM(shape, F32)


def vmem(*arrays):
    return [pltpu.with_memory_space_constraint(a, pltpu.VMEM) for a in arrays]


def triple(m):
    high = lax.reduce_precision(m, 8, 7)
    low = (m - high).astype(BF16)
    high = high.astype(BF16)
    return jnp.concatenate([high, high, low], axis=-2)


def body(
    obs_coef, obs_data, obs_target, leaf_map, leaf_parent, leaf_inv, leaf_off, top_inv, top_rhs
):
    chips = lax.axis_size("chip")
    cores = lax.axis_size("core")
    planes = lax.axis_size("rhs")
    q = lax.axis_index("chip")
    c = lax.axis_index("core")
    local = leaf_inv.shape[0]
    width = leaf_inv.shape[1]
    tops = top_inv.shape[0]
    dates, rows = obs_data.shape
    shard = obs_coef.shape[0]
    total = leaf_map.shape[0]
    slots = cores * CAP
    n_slots = chips * slots
    half = tops // cores
    pieces = half * dates // chips
    span = dates // pieces
    height = dates + shard + 8
    far = far_index(chips)

    payload = pl.pallas_call(
        lambda *refs: join_kernel(*refs, local=local, cores=cores),
        out_shape=arr(height, rows),
        in_specs=[ANY, ANY, ANY, ANY],
        out_specs=VM,
        scratch_shapes=[
            pltpu.VMEM((1, total), I32),
            pltpu.VMEM((1, rows), I32),
            pltpu.SemaphoreType.DMA((4,)),
        ],
        name="join",
    )(leaf_map.reshape(1, total), obs_target.reshape(1, rows), obs_data, obs_coef)
    pair = lax.all_gather(payload, "core", axis=0)
    placed = pl.pallas_call(
        lambda *refs: pack_kernel(*refs, code_row=dates + shard + 1),
        out_shape=arr(n_slots, LANES),
        in_specs=[VM],
        out_specs=VM,
        name="pack",
    )(*vmem(pair))
    recv = exchange(placed.reshape(chips, slots, LANES), "chip", far)

    update_by = triple(jnp.einsum("lcd,lde->lec", leaf_off, leaf_inv, precision=HI))
    product = jnp.einsum("lcd,lde->lce", leaf_off, leaf_inv, precision=HI)
    square = jnp.einsum("ldc,lde->lce", leaf_inv, leaf_inv, precision=HI)
    solve_by = jnp.concatenate([triple(square), triple(-product)], axis=1)
    places = q * (cores * local) + jnp.arange(cores * local, dtype=I32)
    held = leaf_map[None, :] == places[:, None]
    parent = jnp.sum(jnp.where(held, leaf_parent[None, :], 0), axis=1)
    own_parent = lax.dynamic_slice_in_dim(parent, c * local, local, 0)
    parent = jnp.broadcast_to(parent[:, None], (cores * local, LANES))
    own_parent = jnp.broadcast_to(own_parent[:, None], (local, LANES))
    piece = q ^ far
    p = c * half + piece // span
    own_inv = lax.dynamic_index_in_dim(top_inv, p, 0, keepdims=False)
    gram = triple(lax.dot_general(own_inv, own_inv, (((0,), (0,)), ((), ())), precision=HI))
    own_rhs = lax.dynamic_slice(top_rhs, (p, (piece % span) * pieces, 0), (1, pieces, width))
    own_rhs = own_rhs.reshape(pieces, width)
    recv, update_by, solve_by, parent, own_parent, gram, own_rhs = lax.optimization_barrier(
        (recv, update_by, solve_by, parent, own_parent, gram, own_rhs)
    )

    turned, share = pl.pallas_call(
        lambda *refs: turn_kernel(*refs, dates=dates),
        out_shape=(arr(LANES, n_slots), arr(planes, shard, n_slots)),
        in_specs=[VM],
        out_specs=(VM, VM),
        name="turn",
    )(*vmem(recv.reshape(n_slots, LANES)))
    coef = exchange(share, "rhs", planes // 2)
    parts, update = pl.pallas_call(
        lambda *refs: forward_kernel(*refs, shard=shard),
        out_shape=(pltpu.VMEM((local * dates, 3 * width), BF16), arr(local, dates, width)),
        in_specs=[VM, VM, VM],
        out_specs=(VM, VM),
        name="forward",
    )(*vmem(turned, coef, update_by))
    both = lax.all_gather(update, "core", axis=0, tiled=True)
    contrib = pl.pallas_call(
        reduce_kernel,
        out_shape=arr(half, dates, width),
        in_specs=[VM, VM],
        out_specs=VM,
        name="reduce",
    )(*vmem(both, parent))
    got = exchange(contrib.reshape(chips, 1, pieces * width), "chip", far)
    out = pl.pallas_call(
        middle_kernel,
        out_shape=arr(chips * pieces, width),
        in_specs=[VM, VM, VM],
        out_specs=VM,
        name="middle",
    )(*vmem(got.reshape(chips * pieces, width), own_rhs, gram))
    full = exchange(out.reshape(chips, 1, pieces * width), "chip", far)
    full = lax.all_gather(full.reshape(half, dates, width), "core", axis=0, tiled=True)
    return pl.pallas_call(
        last_kernel,
        out_shape=(
            jax.ShapeDtypeStruct((local, dates, width), F32),
            jax.ShapeDtypeStruct((tops, dates, width), F32),
        ),
        in_specs=[VM, VM, VM, VM],
        out_specs=(ANY, ANY),
        scratch_shapes=[
            pltpu.VMEM((local, dates, width), F32),
            pltpu.SemaphoreType.DMA((1 + local,)),
        ],
        name="last",
    )(*vmem(own_parent, full, parts, solve_by))


def solution(mesh):
    devices = mesh.devices
    split = Mesh(devices.reshape(devices.shape[0] // 2, 2, -1), ("chip", "core", "rhs"))
    leaf = ("chip", "core")
    return jax.shard_map(
        body,
        mesh=split,
        in_specs=(
            P("rhs", leaf),
            P("rhs", leaf),
            P(leaf),
            P(),
            P(),
            P(leaf, None, None),
            P(leaf, None, None),
            P(),
            P(None, "rhs", None),
        ),
        out_specs=(P(leaf, "rhs", None), P(None, "rhs", None)),
        check_vma=False,
    )
```

```python
import math

import jax
import jax.numpy as jnp
from jax import lax
from jax.experimental import pallas as pl
from jax.experimental.pallas import tpu as pltpu
from jax.sharding import Mesh, PartitionSpec as P

CAP = 4
LANES = 128
NT = (((1,), (1,)), ((), ()))
NN = (((1,), (0,)), ((), ()))
F32, BF16, I32 = jnp.float32, jnp.bfloat16, jnp.int32


def far_index(count):
    side = math.isqrt(count)
    return side // 2 * side + side // 2


def exchange(x, axis, far):
    order = [i ^ far for i in range(x.shape[0])]
    return lax.all_to_all(x, axis, 0, 0, axis_index_groups=[order])


def split2(x):
    high = x.astype(BF16)
    return high, (x - high.astype(F32)).astype(BF16)


def dot(a, b, dims):
    return lax.dot_general(a, b, dims, preferred_element_type=F32)


def lanes3(m):
    high, low = split2(m)
    return jnp.concatenate([high, high, low], axis=1)


def left3(m):
    high, low = split2(m)
    return jnp.concatenate([high, low, high], axis=1)


def rows3(m):
    high, low = split2(m)
    return jnp.concatenate([high, high, low], axis=0)


def join_kernel(
    map_hbm,
    over_hbm,
    target_hbm,
    data_hbm,
    coef_hbm,
    inv_hbm,
    off_hbm,
    out_ref,
    parent_ref,
    forward_ref,
    back_ref,
    map_ref,
    over_ref,
    target_ref,
    inv_ref,
    off_ref,
    sems,
    *,
    cores,
):
    dates, rows = data_hbm.shape
    shard = coef_hbm.shape[0]
    total = map_hbm.shape[1]
    local = inv_hbm.shape[0]
    copies = [
        pltpu.make_async_copy(map_hbm, map_ref, sems.at[0]),
        pltpu.make_async_copy(target_hbm, target_ref, sems.at[1]),
        pltpu.make_async_copy(inv_hbm, inv_ref, sems.at[2]),
        pltpu.make_async_copy(off_hbm, off_ref, sems.at[3]),
        pltpu.make_async_copy(data_hbm, out_ref.at[pl.ds(0, dates)], sems.at[4]),
        pltpu.make_async_copy(coef_hbm, out_ref.at[pl.ds(dates, shard)], sems.at[5]),
        pltpu.make_async_copy(over_hbm, over_ref, sems.at[6]),
    ]
    for copy in copies:
        copy.start()
    owners = total // local
    chips = owners // cores
    ids = lax.broadcasted_iota(I32, (total, rows), 0)
    owner_ids = lax.broadcasted_iota(I32, (owners, rows), 0)
    before = (
        lax.broadcasted_iota(I32, (rows, rows), 0) < lax.broadcasted_iota(I32, (rows, rows), 1)
    ).astype(F32).astype(BF16)
    copies[0].wait()
    copies[1].wait()
    where_to = map_ref[...]
    table = jnp.concatenate(
        [where_to // local, where_to % local] + [jnp.zeros((1, total), I32)] * 6, axis=0
    ).astype(F32).astype(BF16)
    hit = (ids == target_ref[...]).astype(F32).astype(BF16)
    found = dot(table, hit, NN)
    owner = found[0:1, :].astype(I32)
    same = (owner_ids == owner).astype(F32)
    rank = jnp.sum(same * dot(same.astype(BF16), before, NN), axis=0, keepdims=True)
    slot = ((owner // cores) ^ far_index(chips)) * (cores * CAP) + rank.astype(I32)
    code = (owner % cores) * (chips * cores * CAP) + slot + lax.axis_index("core") * CAP
    tail = out_ref.shape[0] - dates - shard
    out_ref[dates + shard :, :] = jnp.concatenate(
        [found[1:2, :] + 1.0, code.astype(F32), jnp.zeros((tail - 2, rows), F32)], axis=0
    )
    copies[2].wait()
    copies[3].wait()
    for k in range(local):
        inv = inv_ref[k]
        product = dot(left3(off_ref[k]), rows3(inv), NN)
        forward_ref[k] = jnp.concatenate([lanes3(product), lanes3(inv)], axis=0)
        back_ref[k] = jnp.concatenate([rows3(inv), rows3(-product)], axis=0)
    copies[6].wait()
    held = parent_ref.shape[0]
    places = lax.axis_index("chip") * held + lax.broadcasted_iota(I32, (held, total), 0)
    over = jnp.where(where_to == places, over_ref[...], 0).astype(F32)
    parent = jnp.sum(over, axis=1, keepdims=True).astype(I32)
    parent_ref[...] = jnp.broadcast_to(parent, parent_ref.shape)
    copies[4].wait()
    copies[5].wait()


def pack_kernel(pair_ref, out_ref, *, code_row):
    cores, height, rows = pair_ref.shape
    n_slots = out_ref.shape[0]
    code = jnp.concatenate([pair_ref[s, code_row : code_row + 1, :] for s in range(cores)], axis=1)
    code = code.astype(I32) - lax.axis_index("core") * n_slots
    put = (lax.broadcasted_iota(I32, (n_slots, cores * rows), 0) == code).astype(F32).astype(BF16)
    rest = jnp.zeros((LANES - height, cores * rows), F32)
    feat = jnp.concatenate([pair_ref[s] for s in range(cores)], axis=1)
    feat = jnp.concatenate([feat, rest], axis=0)
    both = dot(put, jnp.concatenate(split2(feat), axis=0), NT)
    out_ref[...] = both[:, :LANES] + both[:, LANES:]


def turn_kernel(recv_ref, turned_ref, share_ref, *, dates):
    turned = recv_ref[...].T
    turned_ref[...] = turned
    shard = share_ref.shape[1]
    for i in range(share_ref.shape[0]):
        share_ref[i] = turned[dates : dates + shard, :]


def forward_kernel(turned_ref, coef_ref, by_ref, rows_ref, update_ref, *, shard):
    local, dates, _ = update_ref.shape
    data = turned_ref[0:dates, :]
    mark = turned_ref[dates + shard : dates + shard + 1, :]
    planes = coef_ref.shape[0]
    order = [coef_ref[i ^ (planes // 2)] for i in range(planes)]
    picked = jnp.concatenate(
        [jnp.where(mark == float(k + 1), data, 0.0) for k in range(local)], axis=0
    )
    rhs = left3(dot(left3(picked), lanes3(jnp.concatenate(order, axis=0)), NT))
    width = update_ref.shape[2]
    for k in range(local):
        part = slice(k * dates, (k + 1) * dates)
        both = dot(rhs[part], by_ref[k], NT)
        update_ref[k] = both[:, :width]
        rows_ref[part, :] = left3(both[:, width:])


def reduce_kernel(both_ref, parent_ref, out_ref):
    half, dates, width = out_ref.shape
    first = lax.axis_index("core") * half
    for p in range(half):
        acc = None
        for k in range(both_ref.shape[0]):
            term = jnp.where(parent_ref[k : k + 1, :] == first + p, both_ref[k], 0.0)
            acc = term if acc is None else acc + term
        out_ref[p] = acc


def middle_kernel(got_ref, rhs_ref, inv_ref, out_ref, *, pieces):
    chips = got_ref.shape[0] // pieces
    tops, dates, width = rhs_ref.shape
    half = tops * pieces * chips // (tops * dates)
    span = dates // pieces
    piece = lax.axis_index("chip") ^ far_index(chips)
    p = lax.axis_index("core") * half + piece // span
    sums = [
        jnp.sum(got_ref[pl.ds(k, chips, stride=pieces), :], axis=0, keepdims=True)
        for k in range(pieces)
    ]
    left = rhs_ref[p, pl.ds((piece % span) * pieces, pieces), :] - jnp.concatenate(sums, axis=0)
    left = jnp.concatenate([left, jnp.zeros((8 - pieces % 8, width), F32)], axis=0)
    inv = inv_ref[p]
    sol = dot(left3(dot(left3(left), lanes3(inv), NT)), rows3(inv), NN)
    for k in range(pieces):
        out_ref[pl.ds(k, chips, stride=pieces), :] = jnp.broadcast_to(
            sol[k : k + 1, :], (chips, width)
        )


def last_kernel(parent_ref, top_ref, rows_ref, by_ref, out_hbm, top_hbm, out_ref, sems):
    local, dates, _ = out_ref.shape
    tops = top_ref.shape[0]
    copy_top = pltpu.make_async_copy(top_ref, top_hbm, sems.at[0])
    copy_top.start()
    first = lax.axis_index("core") * local
    copies = []
    for k in range(local):
        parent = parent_ref[pl.ds(first + k, 1), :]
        x = jnp.where(parent == 0, top_ref[0], 0.0)
        for p in range(1, tops):
            x = jnp.where(parent == p, top_ref[p], x)
        rows = rows_ref[k * dates : (k + 1) * dates, :]
        out_ref[k] = dot(jnp.concatenate([rows, left3(x)], axis=1), by_ref[k], NN)
        copies.append(pltpu.make_async_copy(out_ref.at[k], out_hbm.at[k], sems.at[1 + k]))
        copies[-1].start()
    copy_top.wait()
    for copy in copies:
        copy.wait()


VM = pl.BlockSpec(memory_space=pltpu.VMEM)
ANY = pl.BlockSpec(memory_space=pl.ANY)


def arr(*shape):
    return pltpu.VMEM(shape, F32)


def vmem(*arrays):
    return [pltpu.with_memory_space_constraint(a, pltpu.VMEM) for a in arrays]


def body(
    obs_coef, obs_data, obs_target, leaf_map, leaf_parent, leaf_inv, leaf_off, top_inv, top_rhs
):
    chips = lax.axis_size("chip")
    cores = lax.axis_size("core")
    planes = lax.axis_size("rhs")
    local = leaf_inv.shape[0]
    width = leaf_inv.shape[1]
    tops = top_inv.shape[0]
    dates, rows = obs_data.shape
    shard = obs_coef.shape[0]
    total = leaf_map.shape[0]
    slots = cores * CAP
    n_slots = chips * slots
    half = tops // cores
    pieces = half * dates // chips
    height = dates + shard + 8
    far = far_index(chips)

    payload, parent, forward_by, back_by = pl.pallas_call(
        lambda *refs: join_kernel(*refs, cores=cores),
        out_shape=(
            arr(height, rows),
            pltpu.VMEM((cores * local, LANES), I32),
            pltpu.VMEM((local, 2 * width, 3 * width), BF16),
            pltpu.VMEM((local, 6 * width, width), BF16),
        ),
        in_specs=[ANY] * 7,
        out_specs=(VM, VM, VM, VM),
        scratch_shapes=[
            pltpu.VMEM((1, total), I32),
            pltpu.VMEM((1, total), I32),
            pltpu.VMEM((1, rows), I32),
            pltpu.VMEM((local, width, width), F32),
            pltpu.VMEM((local, width, width), F32),
            pltpu.SemaphoreType.DMA((7,)),
        ],
        name="join",
    )(
        leaf_map.reshape(1, total),
        leaf_parent.reshape(1, total),
        obs_target.reshape(1, rows),
        obs_data,
        obs_coef,
        leaf_inv,
        leaf_off,
    )
    pair = lax.all_gather(payload, "core", axis=0)
    placed = pl.pallas_call(
        lambda *refs: pack_kernel(*refs, code_row=dates + shard + 1),
        out_shape=arr(n_slots, LANES),
        in_specs=[VM],
        out_specs=VM,
        name="pack",
    )(*vmem(pair))
    recv = exchange(placed.reshape(chips, slots, LANES), "chip", far)

    turned, share = pl.pallas_call(
        lambda *refs: turn_kernel(*refs, dates=dates),
        out_shape=(arr(LANES, n_slots), arr(planes, shard, n_slots)),
        in_specs=[VM],
        out_specs=(VM, VM),
        name="turn",
    )(*vmem(recv.reshape(n_slots, LANES)))
    coef = exchange(share, "rhs", planes // 2)
    parts, update = pl.pallas_call(
        lambda *refs: forward_kernel(*refs, shard=shard),
        out_shape=(pltpu.VMEM((local * dates, 3 * width), BF16), arr(local, dates, width)),
        in_specs=[VM, VM, VM],
        out_specs=(VM, VM),
        name="forward",
    )(*vmem(turned, coef, forward_by))
    both = lax.all_gather(update, "core", axis=0, tiled=True)
    contrib = pl.pallas_call(
        reduce_kernel,
        out_shape=arr(half, dates, width),
        in_specs=[VM, VM],
        out_specs=VM,
        name="reduce",
    )(*vmem(both, parent))
    got = exchange(contrib.reshape(chips, 1, pieces * width), "chip", far)
    out = pl.pallas_call(
        lambda *refs: middle_kernel(*refs, pieces=pieces),
        out_shape=arr(chips * pieces, width),
        in_specs=[VM, VM, VM],
        out_specs=VM,
        name="middle",
    )(*vmem(got.reshape(chips * pieces, width), top_rhs, top_inv))
    full = exchange(out.reshape(chips, 1, pieces * width), "chip", far)
    full = lax.all_gather(full.reshape(half, dates, width), "core", axis=0, tiled=True)
    return pl.pallas_call(
        last_kernel,
        out_shape=(
            jax.ShapeDtypeStruct((local, dates, width), F32),
            jax.ShapeDtypeStruct((tops, dates, width), F32),
        ),
        in_specs=[VM, VM, VM, VM],
        out_specs=(ANY, ANY),
        scratch_shapes=[
            pltpu.VMEM((local, dates, width), F32),
            pltpu.SemaphoreType.DMA((1 + local,)),
        ],
        name="last",
    )(*vmem(parent, full, parts, back_by))


def solution(mesh):
    devices = mesh.devices
    split = Mesh(devices.reshape(devices.shape[0] // 2, 2, -1), ("chip", "core", "rhs"))
    leaf = ("chip", "core")
    return jax.shard_map(
        body,
        mesh=split,
        in_specs=(
            P("rhs", leaf),
            P("rhs", leaf),
            P(leaf),
            P(),
            P(),
            P(leaf, None, None),
            P(leaf, None, None),
            P(),
            P(None, "rhs", None),
        ),
        out_specs=(P(leaf, "rhs", None), P(None, "rhs", None)),
        check_vma=False,
    )
```

```python
import math

import jax
import jax.numpy as jnp
from jax import lax
from jax.experimental import pallas as pl
from jax.experimental.pallas import tpu as pltpu
from jax.sharding import Mesh, PartitionSpec as P

CAP = 4
LANES = 128
NT = (((1,), (1,)), ((), ()))
NN = (((1,), (0,)), ((), ()))
F32, BF16, I32 = jnp.float32, jnp.bfloat16, jnp.int32


def far_index(count):
    side = math.isqrt(count)
    return side // 2 * side + side // 2


def exchange(x, axis, far):
    order = [i ^ far for i in range(x.shape[0])]
    return lax.all_to_all(x, axis, 0, 0, axis_index_groups=[order])


def split2(x):
    high = x.astype(BF16)
    return high, (x - high.astype(F32)).astype(BF16)


def dot(a, b, dims):
    return lax.dot_general(a, b, dims, preferred_element_type=F32)


def lanes3(m):
    high, low = split2(m)
    return jnp.concatenate([high, high, low], axis=1)


def left3(m):
    high, low = split2(m)
    return jnp.concatenate([high, low, high], axis=1)


def rows3(m):
    high, low = split2(m)
    return jnp.concatenate([high, high, low], axis=0)


def late_start(chips):
    side = math.isqrt(chips)
    q = lax.axis_index("chip")
    return jnp.abs(q // side - side // 2) + jnp.abs(q % side - side // 2) <= side // 2


def fill_back(inv_ref, off_ref, back_ref):
    for k in range(inv_ref.shape[0]):
        inv = inv_ref[k]
        square = dot(left3(inv.T), rows3(inv), NN)
        product = dot(left3(off_ref[k]), rows3(inv), NN)
        back_ref[k] = jnp.concatenate([rows3(square), rows3(-product)], axis=0)


def join_kernel(
    map_hbm,
    over_hbm,
    target_hbm,
    data_hbm,
    coef_hbm,
    inv_hbm,
    off_hbm,
    out_ref,
    parent_ref,
    forward_ref,
    back_ref,
    map_ref,
    over_ref,
    target_ref,
    inv_ref,
    off_ref,
    sems,
    *,
    cores,
):
    dates, rows = data_hbm.shape
    shard = coef_hbm.shape[0]
    total = map_hbm.shape[1]
    local = inv_hbm.shape[0]
    copies = [
        pltpu.make_async_copy(map_hbm, map_ref, sems.at[0]),
        pltpu.make_async_copy(target_hbm, target_ref, sems.at[1]),
        pltpu.make_async_copy(inv_hbm, inv_ref, sems.at[2]),
        pltpu.make_async_copy(off_hbm, off_ref, sems.at[3]),
        pltpu.make_async_copy(data_hbm, out_ref.at[pl.ds(0, dates)], sems.at[4]),
        pltpu.make_async_copy(coef_hbm, out_ref.at[pl.ds(dates, shard)], sems.at[5]),
        pltpu.make_async_copy(over_hbm, over_ref, sems.at[6]),
    ]
    for copy in copies:
        copy.start()
    owners = total // local
    chips = owners // cores
    ids = lax.broadcasted_iota(I32, (total, rows), 0)
    owner_ids = lax.broadcasted_iota(I32, (owners, rows), 0)
    before = (
        lax.broadcasted_iota(I32, (rows, rows), 0) < lax.broadcasted_iota(I32, (rows, rows), 1)
    ).astype(F32).astype(BF16)
    copies[0].wait()
    copies[1].wait()
    where_to = map_ref[...]
    table = jnp.concatenate(
        [where_to // local, where_to % local] + [jnp.zeros((1, total), I32)] * 6, axis=0
    ).astype(F32).astype(BF16)
    hit = (ids == target_ref[...]).astype(F32).astype(BF16)
    found = dot(table, hit, NN)
    owner = found[0:1, :].astype(I32)
    same = (owner_ids == owner).astype(F32)
    rank = jnp.sum(same * dot(same.astype(BF16), before, NN), axis=0, keepdims=True)
    slot = ((owner // cores) ^ far_index(chips)) * (cores * CAP) + rank.astype(I32)
    code = (owner % cores) * (chips * cores * CAP) + slot + lax.axis_index("core") * CAP
    tail = out_ref.shape[0] - dates - shard
    out_ref[dates + shard :, :] = jnp.concatenate(
        [found[1:2, :] + 1.0, code.astype(F32), jnp.zeros((tail - 2, rows), F32)], axis=0
    )
    copies[2].wait()
    copies[3].wait()
    for k in range(local):
        forward_ref[k] = lanes3(dot(left3(off_ref[k]), rows3(inv_ref[k]), NN))
    copies[6].wait()
    held = parent_ref.shape[0]
    places = lax.axis_index("chip") * held + lax.broadcasted_iota(I32, (held, total), 0)
    over = jnp.where(where_to == places, over_ref[...], 0).astype(F32)
    parent = jnp.sum(over, axis=1, keepdims=True).astype(I32)
    parent_ref[...] = jnp.broadcast_to(parent, parent_ref.shape)
    copies[4].wait()
    copies[5].wait()

    @pl.when(jnp.logical_not(late_start(chips)))
    def _():
        fill_back(inv_ref, off_ref, back_ref)


def pack_kernel(pair_ref, out_ref, *, code_row):
    cores, height, rows = pair_ref.shape
    n_slots = out_ref.shape[0]
    code = jnp.concatenate([pair_ref[s, code_row : code_row + 1, :] for s in range(cores)], axis=1)
    code = code.astype(I32) - lax.axis_index("core") * n_slots
    put = (lax.broadcasted_iota(I32, (n_slots, cores * rows), 0) == code).astype(F32).astype(BF16)
    rest = jnp.zeros((LANES - height, cores * rows), F32)
    feat = jnp.concatenate([pair_ref[s] for s in range(cores)], axis=1)
    feat = jnp.concatenate([feat, rest], axis=0)
    both = dot(put, jnp.concatenate(split2(feat), axis=0), NT)
    out_ref[...] = both[:, :LANES] + both[:, LANES:]


def turn_kernel(recv_ref, turned_ref, share_ref, *, dates):
    turned = recv_ref[...].T
    turned_ref[...] = turned
    shard = share_ref.shape[1]
    for i in range(share_ref.shape[0]):
        share_ref[i] = turned[dates : dates + shard, :]


def forward_kernel(turned_ref, coef_ref, by_ref, rows_ref, update_ref, *, shard):
    local, dates, _ = update_ref.shape
    data = turned_ref[0:dates, :]
    mark = turned_ref[dates + shard : dates + shard + 1, :]
    planes = coef_ref.shape[0]
    order = [coef_ref[i ^ (planes // 2)] for i in range(planes)]
    picked = jnp.concatenate(
        [jnp.where(mark == float(k + 1), data, 0.0) for k in range(local)], axis=0
    )
    rhs = left3(dot(left3(picked), lanes3(jnp.concatenate(order, axis=0)), NT))
    rows_ref[...] = rhs
    for k in range(local):
        update_ref[k] = dot(rhs[k * dates : (k + 1) * dates], by_ref[k], NT)


def reduce_kernel(both_ref, parent_ref, out_ref):
    half, dates, width = out_ref.shape
    first = lax.axis_index("core") * half
    for p in range(half):
        acc = None
        for k in range(both_ref.shape[0]):
            term = jnp.where(parent_ref[k : k + 1, :] == first + p, both_ref[k], 0.0)
            acc = term if acc is None else acc + term
        out_ref[p] = acc


def middle_kernel(got_ref, rhs_ref, inv_ref, out_ref, *, pieces):
    chips = got_ref.shape[0] // pieces
    tops, dates, width = rhs_ref.shape
    half = tops * pieces * chips // (tops * dates)
    span = dates // pieces
    piece = lax.axis_index("chip") ^ far_index(chips)
    p = lax.axis_index("core") * half + piece // span
    sums = [
        jnp.sum(got_ref[pl.ds(k, chips, stride=pieces), :], axis=0, keepdims=True)
        for k in range(pieces)
    ]
    left = rhs_ref[p, pl.ds((piece % span) * pieces, pieces), :] - jnp.concatenate(sums, axis=0)
    left = jnp.concatenate([left, jnp.zeros((8 - pieces % 8, width), F32)], axis=0)
    inv = inv_ref[p]
    sol = dot(left3(dot(left3(left), lanes3(inv), NT)), rows3(inv), NN)
    for k in range(pieces):
        out_ref[pl.ds(k, chips, stride=pieces), :] = jnp.broadcast_to(
            sol[k : k + 1, :], (chips, width)
        )


def last_kernel(
    parent_ref,
    top_ref,
    rows_ref,
    back_ref,
    inv_ref,
    off_ref,
    out_hbm,
    top_hbm,
    out_ref,
    own_ref,
    sems,
    *,
    chips,
):
    local, dates, _ = out_ref.shape
    tops = top_ref.shape[0]
    copy_top = pltpu.make_async_copy(top_ref, top_hbm, sems.at[0])
    copy_top.start()
    first = lax.axis_index("core") * local

    def solve(by_ref):
        for k in range(local):
            parent = parent_ref[pl.ds(first + k, 1), :]
            x = jnp.where(parent == 0, top_ref[0], 0.0)
            for p in range(1, tops):
                x = jnp.where(parent == p, top_ref[p], x)
            rows = rows_ref[k * dates : (k + 1) * dates, :]
            out_ref[k] = dot(jnp.concatenate([rows, left3(x)], axis=1), by_ref[k], NN)
            pltpu.make_async_copy(out_ref.at[k], out_hbm.at[k], sems.at[1 + k]).start()

    late = late_start(chips)

    @pl.when(late)
    def _():
        fill_back(inv_ref, off_ref, own_ref)
        solve(own_ref)

    @pl.when(jnp.logical_not(late))
    def _():
        solve(back_ref)

    copy_top.wait()
    for k in range(local):
        pltpu.make_async_copy(out_ref.at[k], out_hbm.at[k], sems.at[1 + k]).wait()


VM = pl.BlockSpec(memory_space=pltpu.VMEM)
ANY = pl.BlockSpec(memory_space=pl.ANY)


def arr(*shape):
    return pltpu.VMEM(shape, F32)


def vmem(*arrays):
    return [pltpu.with_memory_space_constraint(a, pltpu.VMEM) for a in arrays]


def body(
    obs_coef, obs_data, obs_target, leaf_map, leaf_parent, leaf_inv, leaf_off, top_inv, top_rhs
):
    chips = lax.axis_size("chip")
    cores = lax.axis_size("core")
    planes = lax.axis_size("rhs")
    local = leaf_inv.shape[0]
    width = leaf_inv.shape[1]
    tops = top_inv.shape[0]
    dates, rows = obs_data.shape
    shard = obs_coef.shape[0]
    total = leaf_map.shape[0]
    slots = cores * CAP
    n_slots = chips * slots
    half = tops // cores
    pieces = half * dates // chips
    height = dates + shard + 8
    far = far_index(chips)

    payload, parent, forward_by, back_by = pl.pallas_call(
        lambda *refs: join_kernel(*refs, cores=cores),
        out_shape=(
            arr(height, rows),
            pltpu.VMEM((cores * local, LANES), I32),
            pltpu.VMEM((local, width, 3 * width), BF16),
            pltpu.VMEM((local, 6 * width, width), BF16),
        ),
        in_specs=[ANY] * 7,
        out_specs=(VM,) * 4,
        scratch_shapes=[
            pltpu.VMEM((1, total), I32),
            pltpu.VMEM((1, total), I32),
            pltpu.VMEM((1, rows), I32),
            pltpu.VMEM((local, width, width), F32),
            pltpu.VMEM((local, width, width), F32),
            pltpu.SemaphoreType.DMA((7,)),
        ],
        name="join",
    )(
        leaf_map.reshape(1, total),
        leaf_parent.reshape(1, total),
        obs_target.reshape(1, rows),
        obs_data,
        obs_coef,
        leaf_inv,
        leaf_off,
    )
    pair = lax.all_gather(payload, "core", axis=0)
    placed = pl.pallas_call(
        lambda *refs: pack_kernel(*refs, code_row=dates + shard + 1),
        out_shape=arr(n_slots, LANES),
        in_specs=[VM],
        out_specs=VM,
        name="pack",
    )(*vmem(pair))
    recv = exchange(placed.reshape(chips, slots, LANES), "chip", far)

    turned, share = pl.pallas_call(
        lambda *refs: turn_kernel(*refs, dates=dates),
        out_shape=(arr(LANES, n_slots), arr(planes, shard, n_slots)),
        in_specs=[VM],
        out_specs=(VM, VM),
        name="turn",
    )(*vmem(recv.reshape(n_slots, LANES)))
    coef = exchange(share, "rhs", planes // 2)
    parts, update = pl.pallas_call(
        lambda *refs: forward_kernel(*refs, shard=shard),
        out_shape=(pltpu.VMEM((local * dates, 3 * width), BF16), arr(local, dates, width)),
        in_specs=[VM, VM, VM],
        out_specs=(VM, VM),
        name="forward",
    )(*vmem(turned, coef, forward_by))
    both = lax.all_gather(update, "core", axis=0, tiled=True)
    contrib = pl.pallas_call(
        reduce_kernel,
        out_shape=arr(half, dates, width),
        in_specs=[VM, VM],
        out_specs=VM,
        name="reduce",
    )(*vmem(both, parent))
    got = exchange(contrib.reshape(chips, 1, pieces * width), "chip", far)
    out = pl.pallas_call(
        lambda *refs: middle_kernel(*refs, pieces=pieces),
        out_shape=arr(chips * pieces, width),
        in_specs=[VM, VM, VM],
        out_specs=VM,
        name="middle",
    )(*vmem(got.reshape(chips * pieces, width), top_rhs, top_inv))
    full = exchange(out.reshape(chips, 1, pieces * width), "chip", far)
    full = lax.all_gather(full.reshape(half, dates, width), "core", axis=0, tiled=True)
    return pl.pallas_call(
        lambda *refs: last_kernel(*refs, chips=chips),
        out_shape=(
            jax.ShapeDtypeStruct((local, dates, width), F32),
            jax.ShapeDtypeStruct((tops, dates, width), F32),
        ),
        in_specs=[VM] * 6,
        out_specs=(ANY, ANY),
        scratch_shapes=[
            pltpu.VMEM((local, dates, width), F32),
            pltpu.VMEM((local, 6 * width, width), BF16),
            pltpu.SemaphoreType.DMA((1 + local,)),
        ],
        name="last",
    )(*vmem(parent, full, parts, back_by, leaf_inv, leaf_off))


def solution(mesh):
    devices = mesh.devices
    split = Mesh(devices.reshape(devices.shape[0] // 2, 2, -1), ("chip", "core", "rhs"))
    leaf = ("chip", "core")
    return jax.shard_map(
        body,
        mesh=split,
        in_specs=(
            P("rhs", leaf),
            P("rhs", leaf),
            P(leaf),
            P(),
            P(),
            P(leaf, None, None),
            P(leaf, None, None),
            P(),
            P(None, "rhs", None),
        ),
        out_specs=(P(leaf, "rhs", None), P(None, "rhs", None)),
        check_vma=False,
    )
```

```python
import math

import jax
import jax.numpy as jnp
from jax import lax
from jax.experimental import pallas as pl
from jax.experimental.pallas import tpu as pltpu
from jax.sharding import Mesh, PartitionSpec as P

HI = lax.Precision.HIGHEST
CAP = 4
LANES = 128
NT = (((1,), (1,)), ((), ()))
NN = (((1,), (0,)), ((), ()))
F32, BF16, I32 = jnp.float32, jnp.bfloat16, jnp.int32


def far_index(count):
    side = math.isqrt(count)
    return side // 2 * side + side // 2


def exchange(x, axis, far):
    order = [i ^ far for i in range(x.shape[0])]
    return lax.all_to_all(x, axis, 0, 0, axis_index_groups=[order])


def split2(x):
    high = x.astype(BF16)
    return high, (x - high.astype(F32)).astype(BF16)


def dot(a, b, dims):
    return lax.dot_general(a, b, dims, preferred_element_type=F32)


def join_kernel(
    map_hbm,
    target_hbm,
    data_hbm,
    coef_hbm,
    over_hbm,
    out_ref,
    parent_ref,
    map_ref,
    target_ref,
    over_ref,
    sems,
    *,
    local,
    cores,
):
    dates, rows = data_hbm.shape
    shard = coef_hbm.shape[0]
    total = map_hbm.shape[1]
    copies = [
        pltpu.make_async_copy(map_hbm, map_ref, sems.at[0]),
        pltpu.make_async_copy(target_hbm, target_ref, sems.at[1]),
        pltpu.make_async_copy(data_hbm, out_ref.at[pl.ds(0, dates)], sems.at[2]),
        pltpu.make_async_copy(coef_hbm, out_ref.at[pl.ds(dates, shard)], sems.at[3]),
        pltpu.make_async_copy(over_hbm, over_ref, sems.at[4]),
    ]
    for copy in copies:
        copy.start()
    owners = total // local
    chips = owners // cores
    ids = lax.broadcasted_iota(I32, (total, rows), 0)
    owner_ids = lax.broadcasted_iota(I32, (owners, rows), 0)
    before = (
        lax.broadcasted_iota(I32, (rows, rows), 0) < lax.broadcasted_iota(I32, (rows, rows), 1)
    ).astype(F32).astype(BF16)
    copies[0].wait()
    copies[1].wait()
    where_to = map_ref[...]
    table = jnp.concatenate(
        [where_to // local, where_to % local] + [jnp.zeros((1, total), I32)] * 6, axis=0
    ).astype(F32).astype(BF16)
    hit = (ids == target_ref[...]).astype(F32).astype(BF16)
    found = dot(table, hit, NN)
    owner = found[0:1, :].astype(I32)
    same = (owner_ids == owner).astype(F32)
    rank = jnp.sum(same * dot(same.astype(BF16), before, NN), axis=0, keepdims=True)
    slot = ((owner // cores) ^ far_index(chips)) * (cores * CAP) + rank.astype(I32)
    code = (owner % cores) * (chips * cores * CAP) + slot + lax.axis_index("core") * CAP
    tail = out_ref.shape[0] - dates - shard
    out_ref[dates + shard :, :] = jnp.concatenate(
        [found[1:2, :] + 1.0, code.astype(F32), jnp.zeros((tail - 2, rows), F32)], axis=0
    )
    copies[4].wait()
    held = parent_ref.shape[0]
    places = lax.axis_index("chip") * held + lax.broadcasted_iota(I32, (held, total), 0)
    over = jnp.where(where_to == places, over_ref[...], 0).astype(F32)
    parent = jnp.sum(over, axis=1, keepdims=True).astype(I32)
    parent_ref[...] = jnp.broadcast_to(parent, parent_ref.shape)
    copies[2].wait()
    copies[3].wait()


def pack_kernel(pair_ref, out_hbm, out_ref, sems, *, code_row):
    cores, height, rows = pair_ref.shape
    n_slots = out_ref.shape[0]
    parts = sems.shape[0]
    size = n_slots // parts
    code = jnp.concatenate([pair_ref[s, code_row : code_row + 1, :] for s in range(cores)], axis=1)
    code = code.astype(I32) - lax.axis_index("core") * n_slots
    rest = jnp.zeros((LANES - height, cores * rows), F32)
    feat = jnp.concatenate([pair_ref[s] for s in range(cores)], axis=1)
    feat = jnp.concatenate(split2(jnp.concatenate([feat, rest], axis=0)), axis=0)
    ids = lax.broadcasted_iota(I32, (size, cores * rows), 0)
    copies = []
    for i in range(parts):
        put = (ids == code - i * size).astype(F32).astype(BF16)
        both = dot(put, feat, NT)
        here = pl.ds(i * size, size)
        out_ref[here, :] = both[:, :LANES] + both[:, LANES:]
        copies.append(pltpu.make_async_copy(out_ref.at[here], out_hbm.at[here], sems.at[i]))
        copies[-1].start()
    for copy in copies:
        copy.wait()


def turn_kernel(recv_ref, turned_ref, share_ref, *, dates):
    turned = recv_ref[...].T
    turned_ref[...] = turned
    shard = share_ref.shape[1]
    for i in range(share_ref.shape[0]):
        share_ref[i] = turned[dates : dates + shard, :]


def forward_kernel(turned_ref, coef_ref, comb_ref, rows_ref, update_ref, *, shard):
    local, dates, _ = update_ref.shape
    data = turned_ref[0:dates, :]
    mark = turned_ref[dates + shard : dates + shard + 1, :]
    planes = coef_ref.shape[0]
    order = [coef_ref[i ^ (planes // 2)] for i in range(planes)]
    coef_high, coef_low = split2(jnp.concatenate(order, axis=0))
    coef = jnp.concatenate([coef_high, coef_high, coef_low], axis=1)
    picked = jnp.concatenate(
        [jnp.where(mark == float(k + 1), data, 0.0) for k in range(local)], axis=0
    )
    high, low = split2(picked)
    rhs = dot(jnp.concatenate([high, low, high], axis=1), coef, NT)
    high, low = split2(rhs)
    rows = jnp.concatenate([high, low, high], axis=1)
    rows_ref[...] = rows
    for k in range(local):
        update_ref[k] = dot(rows[k * dates : (k + 1) * dates], comb_ref[k], NN)


def reduce_kernel(both_ref, parent_ref, out_ref):
    half, dates, width = out_ref.shape
    first = lax.axis_index("core") * half
    for p in range(half):
        acc = None
        for k in range(both_ref.shape[0]):
            term = jnp.where(parent_ref[k : k + 1, :] == first + p, both_ref[k], 0.0)
            acc = term if acc is None else acc + term
        out_ref[p] = acc


def middle_kernel(got_ref, rhs_ref, gram_ref, out_ref):
    pieces, width = rhs_ref.shape
    chips = got_ref.shape[0] // pieces
    sums = [
        jnp.sum(got_ref[pl.ds(k, chips, stride=pieces), :], axis=0, keepdims=True)
        for k in range(pieces)
    ]
    left = rhs_ref[...] - jnp.concatenate(sums, axis=0)
    left = jnp.concatenate([left, jnp.zeros((8 - pieces % 8, width), F32)], axis=0)
    high, low = split2(left)
    sol = dot(jnp.concatenate([high, low, high], axis=1), gram_ref[...], NN)
    for k in range(pieces):
        out_ref[pl.ds(k, chips, stride=pieces), :] = jnp.broadcast_to(
            sol[k : k + 1, :], (chips, width)
        )


def last_kernel(parent_ref, top_ref, rows_ref, both_ref, out_hbm, top_hbm, out_ref, sems):
    local, dates, _ = out_ref.shape
    tops = top_ref.shape[0]
    copy_top = pltpu.make_async_copy(top_ref, top_hbm, sems.at[0])
    copy_top.start()
    first = lax.axis_index("core") * local
    copies = []
    for k in range(local):
        parent = parent_ref[pl.ds(first + k, 1), :]
        x = jnp.where(parent == 0, top_ref[0], 0.0)
        for p in range(1, tops):
            x = jnp.where(parent == p, top_ref[p], x)
        high, low = split2(x)
        rows = rows_ref[k * dates : (k + 1) * dates, :]
        out_ref[k] = dot(jnp.concatenate([rows, high, low, high], axis=1), both_ref[k], NN)
        copies.append(pltpu.make_async_copy(out_ref.at[k], out_hbm.at[k], sems.at[1 + k]))
        copies[-1].start()
    copy_top.wait()
    for copy in copies:
        copy.wait()


VM = pl.BlockSpec(memory_space=pltpu.VMEM)
ANY = pl.BlockSpec(memory_space=pl.ANY)


def arr(*shape):
    return pltpu.VMEM(shape, F32)


def vmem(*arrays):
    return [pltpu.with_memory_space_constraint(a, pltpu.VMEM) for a in arrays]


def triple(m):
    high = lax.reduce_precision(m, 8, 7)
    low = (m - high).astype(BF16)
    high = high.astype(BF16)
    return jnp.concatenate([high, high, low], axis=-2)


def body(
    obs_coef, obs_data, obs_target, leaf_map, leaf_parent, leaf_inv, leaf_off, top_inv, top_rhs
):
    chips = lax.axis_size("chip")
    cores = lax.axis_size("core")
    planes = lax.axis_size("rhs")
    q = lax.axis_index("chip")
    c = lax.axis_index("core")
    local = leaf_inv.shape[0]
    width = leaf_inv.shape[1]
    tops = top_inv.shape[0]
    dates, rows = obs_data.shape
    shard = obs_coef.shape[0]
    total = leaf_map.shape[0]
    slots = cores * CAP
    n_slots = chips * slots
    half = tops // cores
    pieces = half * dates // chips
    span = dates // pieces
    height = dates + shard + 8
    far = far_index(chips)

    payload, parent = pl.pallas_call(
        lambda *refs: join_kernel(*refs, local=local, cores=cores),
        out_shape=(arr(height, rows), pltpu.VMEM((cores * local, LANES), I32)),
        in_specs=[ANY] * 5,
        out_specs=(VM, VM),
        scratch_shapes=[
            pltpu.VMEM((1, total), I32),
            pltpu.VMEM((1, rows), I32),
            pltpu.VMEM((1, total), I32),
            pltpu.SemaphoreType.DMA((5,)),
        ],
        name="join",
    )(
        leaf_map.reshape(1, total),
        obs_target.reshape(1, rows),
        obs_data,
        obs_coef,
        leaf_parent.reshape(1, total),
    )
    pair = lax.all_gather(payload, "core", axis=0)
    placed = pl.pallas_call(
        lambda *refs: pack_kernel(*refs, code_row=dates + shard + 1),
        out_shape=jax.ShapeDtypeStruct((n_slots, LANES), F32),
        in_specs=[VM],
        out_specs=ANY,
        scratch_shapes=[pltpu.VMEM((n_slots, LANES), F32), pltpu.SemaphoreType.DMA((4,))],
        name="pack",
    )(*vmem(pair))
    recv = exchange(placed.reshape(chips, slots, LANES), "chip", far)

    update_by = triple(jnp.einsum("lcd,lde->lec", leaf_off, leaf_inv, precision=HI))
    product = jnp.einsum("lcd,lde->lce", leaf_off, leaf_inv, precision=HI)
    square = jnp.einsum("ldc,lde->lce", leaf_inv, leaf_inv, precision=HI)
    solve_by = jnp.concatenate([triple(square), triple(-product)], axis=1)
    piece = q ^ far
    p = c * half + piece // span
    own_inv = lax.dynamic_index_in_dim(top_inv, p, 0, keepdims=False)
    gram = triple(lax.dot_general(own_inv, own_inv, (((0,), (0,)), ((), ())), precision=HI))
    own_rhs = lax.dynamic_slice(top_rhs, (p, (piece % span) * pieces, 0), (1, pieces, width))
    own_rhs = own_rhs.reshape(pieces, width)
    recv, update_by, solve_by, gram, own_rhs = lax.optimization_barrier(
        (recv, update_by, solve_by, gram, own_rhs)
    )

    turned, share = pl.pallas_call(
        lambda *refs: turn_kernel(*refs, dates=dates),
        out_shape=(arr(LANES, n_slots), arr(planes, shard, n_slots)),
        in_specs=[VM],
        out_specs=(VM, VM),
        name="turn",
    )(*vmem(recv.reshape(n_slots, LANES)))
    coef = exchange(share, "rhs", planes // 2)
    parts, update = pl.pallas_call(
        lambda *refs: forward_kernel(*refs, shard=shard),
        out_shape=(pltpu.VMEM((local * dates, 3 * width), BF16), arr(local, dates, width)),
        in_specs=[VM, VM, VM],
        out_specs=(VM, VM),
        name="forward",
    )(*vmem(turned, coef, update_by))
    both = lax.all_gather(update, "core", axis=0, tiled=True)
    contrib = pl.pallas_call(
        reduce_kernel,
        out_shape=arr(half, dates, width),
        in_specs=[VM, VM],
        out_specs=VM,
        name="reduce",
    )(*vmem(both, parent))
    got = exchange(contrib.reshape(chips, 1, pieces * width), "chip", far)
    out = pl.pallas_call(
        middle_kernel,
        out_shape=arr(chips * pieces, width),
        in_specs=[VM, VM, VM],
        out_specs=VM,
        name="middle",
    )(*vmem(got.reshape(chips * pieces, width), own_rhs, gram))
    full = exchange(out.reshape(chips, 1, pieces * width), "chip", far)
    full = lax.all_gather(full.reshape(half, dates, width), "core", axis=0, tiled=True)
    return pl.pallas_call(
        last_kernel,
        out_shape=(
            jax.ShapeDtypeStruct((local, dates, width), F32),
            jax.ShapeDtypeStruct((tops, dates, width), F32),
        ),
        in_specs=[VM, VM, VM, VM],
        out_specs=(ANY, ANY),
        scratch_shapes=[
            pltpu.VMEM((local, dates, width), F32),
            pltpu.SemaphoreType.DMA((1 + local,)),
        ],
        name="last",
    )(*vmem(parent, full, parts, solve_by))


def solution(mesh):
    devices = mesh.devices
    split = Mesh(devices.reshape(devices.shape[0] // 2, 2, -1), ("chip", "core", "rhs"))
    leaf = ("chip", "core")
    return jax.shard_map(
        body,
        mesh=split,
        in_specs=(
            P("rhs", leaf),
            P("rhs", leaf),
            P(leaf),
            P(),
            P(),
            P(leaf, None, None),
            P(leaf, None, None),
            P(),
            P(None, "rhs", None),
        ),
        out_specs=(P(leaf, "rhs", None), P(None, "rhs", None)),
        check_vma=False,
    )
```

```python
import math

import jax
import jax.numpy as jnp
from jax import lax
from jax.experimental import pallas as pl
from jax.experimental.pallas import tpu as pltpu
from jax.sharding import Mesh, PartitionSpec as P

CAP = 4
LANES = 128
NT = (((1,), (1,)), ((), ()))
NN = (((1,), (0,)), ((), ()))
F32, BF16, I32 = jnp.float32, jnp.bfloat16, jnp.int32


def far_index(count):
    side = math.isqrt(count)
    return side // 2 * side + side // 2


def exchange(x, axis, far):
    order = [i ^ far for i in range(x.shape[0])]
    return lax.all_to_all(x, axis, 0, 0, axis_index_groups=[order])


def split2(x):
    high = x.astype(BF16)
    return high, (x - high.astype(F32)).astype(BF16)


def dot(a, b, dims):
    return lax.dot_general(a, b, dims, preferred_element_type=F32)


def lanes3(m):
    high, low = split2(m)
    return jnp.concatenate([high, high, low], axis=1)


def left3(m):
    high, low = split2(m)
    return jnp.concatenate([high, low, high], axis=1)


def rows3(m):
    high, low = split2(m)
    return jnp.concatenate([high, high, low], axis=0)


def late_start(chips):
    side = math.isqrt(chips)
    q = lax.axis_index("chip")
    return jnp.abs(q // side - side // 2) + jnp.abs(q % side - side // 2) <= side // 2


def fill_back(inv_ref, off_ref, back_ref):
    for k in range(inv_ref.shape[0]):
        inv = inv_ref[k]
        square = dot(left3(inv.T), rows3(inv), NN)
        product = dot(left3(off_ref[k]), rows3(inv), NN)
        back_ref[k] = jnp.concatenate([rows3(square), rows3(-product)], axis=0)


def join_kernel(
    map_hbm,
    over_hbm,
    target_hbm,
    data_hbm,
    coef_hbm,
    inv_hbm,
    off_hbm,
    out_ref,
    parent_ref,
    forward_ref,
    back_ref,
    map_ref,
    over_ref,
    target_ref,
    inv_ref,
    off_ref,
    sems,
    *,
    cores,
):
    dates, rows = data_hbm.shape
    shard = coef_hbm.shape[0]
    total = map_hbm.shape[1]
    local = inv_hbm.shape[0]
    copies = [
        pltpu.make_async_copy(map_hbm, map_ref, sems.at[0]),
        pltpu.make_async_copy(target_hbm, target_ref, sems.at[1]),
        pltpu.make_async_copy(inv_hbm, inv_ref, sems.at[2]),
        pltpu.make_async_copy(off_hbm, off_ref, sems.at[3]),
        pltpu.make_async_copy(data_hbm, out_ref.at[pl.ds(0, dates)], sems.at[4]),
        pltpu.make_async_copy(coef_hbm, out_ref.at[pl.ds(dates, shard)], sems.at[5]),
        pltpu.make_async_copy(over_hbm, over_ref, sems.at[6]),
    ]
    for copy in copies:
        copy.start()
    owners = total // local
    chips = owners // cores
    ids = lax.broadcasted_iota(I32, (total, rows), 0)
    owner_ids = lax.broadcasted_iota(I32, (owners, rows), 0)
    before = (
        lax.broadcasted_iota(I32, (rows, rows), 0) < lax.broadcasted_iota(I32, (rows, rows), 1)
    ).astype(F32).astype(BF16)
    copies[0].wait()
    copies[1].wait()
    where_to = map_ref[...]
    table = jnp.concatenate(
        [where_to // local, where_to % local] + [jnp.zeros((1, total), I32)] * 6, axis=0
    ).astype(F32).astype(BF16)
    hit = (ids == target_ref[...]).astype(F32).astype(BF16)
    found = dot(table, hit, NN)
    owner = found[0:1, :].astype(I32)
    same = (owner_ids == owner).astype(F32)
    rank = jnp.sum(same * dot(same.astype(BF16), before, NN), axis=0, keepdims=True)
    slot = ((owner // cores) ^ far_index(chips)) * (cores * CAP) + rank.astype(I32)
    code = (owner % cores) * (chips * cores * CAP) + slot + lax.axis_index("core") * CAP
    tail = out_ref.shape[0] - dates - shard
    out_ref[dates + shard :, :] = jnp.concatenate(
        [found[1:2, :] + 1.0, code.astype(F32), jnp.zeros((tail - 2, rows), F32)], axis=0
    )
    copies[2].wait()
    copies[3].wait()
    for k in range(local):
        forward_ref[k] = lanes3(dot(left3(off_ref[k]), rows3(inv_ref[k]), NN))
    copies[6].wait()
    held = parent_ref.shape[0]
    places = lax.axis_index("chip") * held + lax.broadcasted_iota(I32, (held, total), 0)
    over = jnp.where(where_to == places, over_ref[...], 0).astype(F32)
    parent = jnp.sum(over, axis=1, keepdims=True).astype(I32)
    parent_ref[...] = jnp.broadcast_to(parent, parent_ref.shape)
    copies[4].wait()
    copies[5].wait()

    @pl.when(jnp.logical_not(late_start(chips)))
    def _():
        fill_back(inv_ref, off_ref, back_ref)


def pack_kernel(pair_ref, out_ref, *, code_row):
    cores, height, rows = pair_ref.shape
    n_slots = out_ref.shape[0]
    code = jnp.concatenate([pair_ref[s, code_row : code_row + 1, :] for s in range(cores)], axis=1)
    code = code.astype(I32) - lax.axis_index("core") * n_slots
    put = (lax.broadcasted_iota(I32, (n_slots, cores * rows), 0) == code).astype(F32).astype(BF16)
    rest = jnp.zeros((LANES - height, cores * rows), F32)
    feat = jnp.concatenate([pair_ref[s] for s in range(cores)], axis=1)
    feat = jnp.concatenate([feat, rest], axis=0)
    both = dot(put, jnp.concatenate(split2(feat), axis=0), NT)
    out_ref[...] = both[:, :LANES] + both[:, LANES:]


def turn_kernel(recv_ref, turned_ref, share_ref, *, dates):
    turned = recv_ref[...].T
    turned_ref[...] = turned
    shard = share_ref.shape[1]
    for i in range(share_ref.shape[0]):
        share_ref[i] = turned[dates : dates + shard, :]


def forward_kernel(turned_ref, coef_ref, by_ref, rows_ref, update_ref, *, shard):
    local, dates, _ = update_ref.shape
    data = turned_ref[0:dates, :]
    mark = turned_ref[dates + shard : dates + shard + 1, :]
    planes = coef_ref.shape[0]
    order = [coef_ref[i ^ (planes // 2)] for i in range(planes)]
    picked = jnp.concatenate(
        [jnp.where(mark == float(k + 1), data, 0.0) for k in range(local)], axis=0
    )
    rhs = left3(dot(left3(picked), lanes3(jnp.concatenate(order, axis=0)), NT))
    rows_ref[...] = rhs
    for k in range(local):
        update_ref[k] = dot(rhs[k * dates : (k + 1) * dates], by_ref[k], NT)


def reduce_kernel(both_ref, parent_ref, out_ref):
    half, dates, width = out_ref.shape
    first = lax.axis_index("core") * half
    for p in range(half):
        acc = None
        for k in range(both_ref.shape[0]):
            term = jnp.where(parent_ref[k : k + 1, :] == first + p, both_ref[k], 0.0)
            acc = term if acc is None else acc + term
        out_ref[p] = acc


def middle_kernel(got_ref, rhs_ref, inv_ref, out_ref, *, pieces):
    chips = got_ref.shape[0] // pieces
    tops, dates, width = rhs_ref.shape
    half = tops * pieces * chips // (tops * dates)
    span = dates // pieces
    piece = lax.axis_index("chip") ^ far_index(chips)
    p = lax.axis_index("core") * half + piece // span
    sums = [
        jnp.sum(got_ref[pl.ds(k, chips, stride=pieces), :], axis=0, keepdims=True)
        for k in range(pieces)
    ]
    left = rhs_ref[p, pl.ds((piece % span) * pieces, pieces), :] - jnp.concatenate(sums, axis=0)
    left = jnp.concatenate([left, jnp.zeros((8 - pieces % 8, width), F32)], axis=0)
    inv = inv_ref[p]
    sol = dot(left3(dot(left3(left), lanes3(inv), NT)), rows3(inv), NN)
    for k in range(pieces):
        out_ref[pl.ds(k, chips, stride=pieces), :] = jnp.broadcast_to(
            sol[k : k + 1, :], (chips, width)
        )


def last_kernel(
    parent_ref,
    top_ref,
    rows_ref,
    back_ref,
    inv_hbm,
    off_hbm,
    out_hbm,
    top_hbm,
    out_ref,
    own_ref,
    inv_ref,
    off_ref,
    sems,
    *,
    chips,
):
    local, dates, _ = out_ref.shape
    tops = top_ref.shape[0]
    copy_top = pltpu.make_async_copy(top_ref, top_hbm, sems.at[0])
    copy_top.start()
    first = lax.axis_index("core") * local

    def solve(by_ref):
        for k in range(local):
            parent = parent_ref[pl.ds(first + k, 1), :]
            x = jnp.where(parent == 0, top_ref[0], 0.0)
            for p in range(1, tops):
                x = jnp.where(parent == p, top_ref[p], x)
            rows = rows_ref[k * dates : (k + 1) * dates, :]
            out_ref[k] = dot(jnp.concatenate([rows, left3(x)], axis=1), by_ref[k], NN)
            pltpu.make_async_copy(out_ref.at[k], out_hbm.at[k], sems.at[1 + k]).start()

    late = late_start(chips)

    @pl.when(late)
    def _():
        get_inv = pltpu.make_async_copy(inv_hbm, inv_ref, sems.at[1 + local])
        get_off = pltpu.make_async_copy(off_hbm, off_ref, sems.at[2 + local])
        get_inv.start()
        get_off.start()
        get_inv.wait()
        get_off.wait()
        fill_back(inv_ref, off_ref, own_ref)
        solve(own_ref)

    @pl.when(jnp.logical_not(late))
    def _():
        solve(back_ref)

    copy_top.wait()
    for k in range(local):
        pltpu.make_async_copy(out_ref.at[k], out_hbm.at[k], sems.at[1 + k]).wait()


VM = pl.BlockSpec(memory_space=pltpu.VMEM)
ANY = pl.BlockSpec(memory_space=pl.ANY)


def arr(*shape):
    return pltpu.VMEM(shape, F32)


def vmem(*arrays):
    return [pltpu.with_memory_space_constraint(a, pltpu.VMEM) for a in arrays]


def body(
    obs_coef, obs_data, obs_target, leaf_map, leaf_parent, leaf_inv, leaf_off, top_inv, top_rhs
):
    chips = lax.axis_size("chip")
    cores = lax.axis_size("core")
    planes = lax.axis_size("rhs")
    local = leaf_inv.shape[0]
    width = leaf_inv.shape[1]
    tops = top_inv.shape[0]
    dates, rows = obs_data.shape
    shard = obs_coef.shape[0]
    total = leaf_map.shape[0]
    slots = cores * CAP
    n_slots = chips * slots
    half = tops // cores
    pieces = half * dates // chips
    height = dates + shard + 8
    far = far_index(chips)

    payload, parent, forward_by, back_by = pl.pallas_call(
        lambda *refs: join_kernel(*refs, cores=cores),
        out_shape=(
            arr(height, rows),
            pltpu.VMEM((cores * local, LANES), I32),
            pltpu.VMEM((local, width, 3 * width), BF16),
            pltpu.VMEM((local, 6 * width, width), BF16),
        ),
        in_specs=[ANY] * 7,
        out_specs=(VM,) * 4,
        scratch_shapes=[
            pltpu.VMEM((1, total), I32),
            pltpu.VMEM((1, total), I32),
            pltpu.VMEM((1, rows), I32),
            pltpu.VMEM((local, width, width), F32),
            pltpu.VMEM((local, width, width), F32),
            pltpu.SemaphoreType.DMA((7,)),
        ],
        name="join",
    )(
        leaf_map.reshape(1, total),
        leaf_parent.reshape(1, total),
        obs_target.reshape(1, rows),
        obs_data,
        obs_coef,
        leaf_inv,
        leaf_off,
    )
    pair = lax.all_gather(payload, "core", axis=0)
    placed = pl.pallas_call(
        lambda *refs: pack_kernel(*refs, code_row=dates + shard + 1),
        out_shape=arr(n_slots, LANES),
        in_specs=[VM],
        out_specs=VM,
        name="pack",
    )(*vmem(pair))
    recv = exchange(placed.reshape(chips, slots, LANES), "chip", far)

    turned, share = pl.pallas_call(
        lambda *refs: turn_kernel(*refs, dates=dates),
        out_shape=(arr(LANES, n_slots), arr(planes, shard, n_slots)),
        in_specs=[VM],
        out_specs=(VM, VM),
        name="turn",
    )(*vmem(recv.reshape(n_slots, LANES)))
    coef = exchange(share, "rhs", planes // 2)
    parts, update = pl.pallas_call(
        lambda *refs: forward_kernel(*refs, shard=shard),
        out_shape=(pltpu.VMEM((local * dates, 3 * width), BF16), arr(local, dates, width)),
        in_specs=[VM, VM, VM],
        out_specs=(VM, VM),
        name="forward",
    )(*vmem(turned, coef, forward_by))
    both = lax.all_gather(update, "core", axis=0, tiled=True)
    contrib = pl.pallas_call(
        reduce_kernel,
        out_shape=arr(half, dates, width),
        in_specs=[VM, VM],
        out_specs=VM,
        name="reduce",
    )(*vmem(both, parent))
    got = exchange(contrib.reshape(chips, 1, pieces * width), "chip", far)
    out = pl.pallas_call(
        lambda *refs: middle_kernel(*refs, pieces=pieces),
        out_shape=arr(chips * pieces, width),
        in_specs=[VM, VM, VM],
        out_specs=VM,
        name="middle",
    )(*vmem(got.reshape(chips * pieces, width), top_rhs, top_inv))
    full = exchange(out.reshape(chips, 1, pieces * width), "chip", far)
    full = lax.all_gather(full.reshape(half, dates, width), "core", axis=0, tiled=True)
    return pl.pallas_call(
        lambda *refs: last_kernel(*refs, chips=chips),
        out_shape=(
            jax.ShapeDtypeStruct((local, dates, width), F32),
            jax.ShapeDtypeStruct((tops, dates, width), F32),
        ),
        in_specs=[VM, VM, VM, VM, ANY, ANY],
        out_specs=(ANY, ANY),
        scratch_shapes=[
            pltpu.VMEM((local, dates, width), F32),
            pltpu.VMEM((local, 6 * width, width), BF16),
            pltpu.VMEM((local, width, width), F32),
            pltpu.VMEM((local, width, width), F32),
            pltpu.SemaphoreType.DMA((3 + local,)),
        ],
        name="last",
    )(*vmem(parent, full, parts, back_by), leaf_inv, leaf_off)


def solution(mesh):
    devices = mesh.devices
    split = Mesh(devices.reshape(devices.shape[0] // 2, 2, -1), ("chip", "core", "rhs"))
    leaf = ("chip", "core")
    return jax.shard_map(
        body,
        mesh=split,
        in_specs=(
            P("rhs", leaf),
            P("rhs", leaf),
            P(leaf),
            P(),
            P(),
            P(leaf, None, None),
            P(leaf, None, None),
            P(),
            P(None, "rhs", None),
        ),
        out_specs=(P(leaf, "rhs", None), P(None, "rhs", None)),
        check_vma=False,
    )
```

```python
import math

import jax
import jax.numpy as jnp
from jax import lax
from jax.experimental import pallas as pl
from jax.experimental.pallas import tpu as pltpu
from jax.sharding import Mesh, PartitionSpec as P

CAP = 4
LANES = 128
NT = (((1,), (1,)), ((), ()))
NN = (((1,), (0,)), ((), ()))
F32, BF16, I32 = jnp.float32, jnp.bfloat16, jnp.int32


def far_index(count):
    side = math.isqrt(count)
    return side // 2 * side + side // 2 + 1


def exchange(x, axis, far):
    order = [i ^ far for i in range(x.shape[0])]
    return lax.all_to_all(x, axis, 0, 0, axis_index_groups=[order])


def split2(x):
    high = x.astype(BF16)
    return high, (x - high.astype(F32)).astype(BF16)


def dot(a, b, dims):
    return lax.dot_general(a, b, dims, preferred_element_type=F32)


def lanes3(m):
    high, low = split2(m)
    return jnp.concatenate([high, high, low], axis=1)


def left3(m):
    high, low = split2(m)
    return jnp.concatenate([high, low, high], axis=1)


def rows3(m):
    high, low = split2(m)
    return jnp.concatenate([high, high, low], axis=0)


def join_kernel(
    map_hbm,
    over_hbm,
    target_hbm,
    data_hbm,
    coef_hbm,
    inv_hbm,
    off_hbm,
    out_ref,
    parent_ref,
    forward_ref,
    back_ref,
    map_ref,
    over_ref,
    target_ref,
    inv_ref,
    off_ref,
    sems,
    *,
    cores,
):
    dates, rows = data_hbm.shape
    shard = coef_hbm.shape[0]
    total = map_hbm.shape[1]
    local = inv_hbm.shape[0]
    copies = [
        pltpu.make_async_copy(map_hbm, map_ref, sems.at[0]),
        pltpu.make_async_copy(target_hbm, target_ref, sems.at[1]),
        pltpu.make_async_copy(inv_hbm, inv_ref, sems.at[2]),
        pltpu.make_async_copy(off_hbm, off_ref, sems.at[3]),
        pltpu.make_async_copy(data_hbm, out_ref.at[pl.ds(0, dates)], sems.at[4]),
        pltpu.make_async_copy(coef_hbm, out_ref.at[pl.ds(dates, shard)], sems.at[5]),
        pltpu.make_async_copy(over_hbm, over_ref, sems.at[6]),
    ]
    for copy in copies:
        copy.start()
    owners = total // local
    chips = owners // cores
    ids = lax.broadcasted_iota(I32, (total, rows), 0)
    owner_ids = lax.broadcasted_iota(I32, (owners, rows), 0)
    before = (
        lax.broadcasted_iota(I32, (rows, rows), 0) < lax.broadcasted_iota(I32, (rows, rows), 1)
    ).astype(F32).astype(BF16)
    copies[0].wait()
    copies[1].wait()
    where_to = map_ref[...]
    table = jnp.concatenate(
        [where_to // local, where_to % local] + [jnp.zeros((1, total), I32)] * 6, axis=0
    ).astype(F32).astype(BF16)
    hit = (ids == target_ref[...]).astype(F32).astype(BF16)
    found = dot(table, hit, NN)
    owner = found[0:1, :].astype(I32)
    same = (owner_ids == owner).astype(F32)
    rank = jnp.sum(same * dot(same.astype(BF16), before, NN), axis=0, keepdims=True)
    slot = ((owner // cores) ^ far_index(chips)) * (cores * CAP) + rank.astype(I32)
    code = (owner % cores) * (chips * cores * CAP) + slot + lax.axis_index("core") * CAP
    tail = out_ref.shape[0] - dates - shard
    out_ref[dates + shard :, :] = jnp.concatenate(
        [found[1:2, :] + 1.0, code.astype(F32), jnp.zeros((tail - 2, rows), F32)], axis=0
    )
    copies[2].wait()
    copies[3].wait()
    for k in range(local):
        inv = inv_ref[k]
        product = dot(left3(off_ref[k]), rows3(inv), NN)
        forward_ref[k] = jnp.concatenate([lanes3(product), lanes3(inv)], axis=0)
        back_ref[k] = jnp.concatenate([rows3(inv), rows3(-product)], axis=0)
    copies[6].wait()
    held = parent_ref.shape[0]
    places = lax.axis_index("chip") * held + lax.broadcasted_iota(I32, (held, total), 0)
    over = jnp.where(where_to == places, over_ref[...], 0).astype(F32)
    parent = jnp.sum(over, axis=1, keepdims=True).astype(I32)
    parent_ref[...] = jnp.broadcast_to(parent, parent_ref.shape)
    copies[4].wait()
    copies[5].wait()


def pack_kernel(pair_ref, out_ref, *, code_row):
    cores, height, rows = pair_ref.shape
    n_slots = out_ref.shape[0]
    code = jnp.concatenate([pair_ref[s, code_row : code_row + 1, :] for s in range(cores)], axis=1)
    code = code.astype(I32) - lax.axis_index("core") * n_slots
    put = (lax.broadcasted_iota(I32, (n_slots, cores * rows), 0) == code).astype(F32).astype(BF16)
    rest = jnp.zeros((LANES - height, cores * rows), F32)
    feat = jnp.concatenate([pair_ref[s] for s in range(cores)], axis=1)
    feat = jnp.concatenate([feat, rest], axis=0)
    both = dot(put, jnp.concatenate(split2(feat), axis=0), NT)
    out_ref[...] = both[:, :LANES] + both[:, LANES:]


def turn_kernel(recv_ref, turned_ref, share_ref, *, dates):
    turned = recv_ref[...].T
    turned_ref[...] = turned
    shard = share_ref.shape[1]
    for i in range(share_ref.shape[0]):
        share_ref[i] = turned[dates : dates + shard, :]


def forward_kernel(turned_ref, coef_ref, by_ref, rows_ref, update_ref, *, shard):
    local, dates, _ = update_ref.shape
    data = turned_ref[0:dates, :]
    mark = turned_ref[dates + shard : dates + shard + 1, :]
    planes = coef_ref.shape[0]
    order = [coef_ref[i ^ (planes // 2)] for i in range(planes)]
    picked = jnp.concatenate(
        [jnp.where(mark == float(k + 1), data, 0.0) for k in range(local)], axis=0
    )
    rhs = left3(dot(left3(picked), lanes3(jnp.concatenate(order, axis=0)), NT))
    width = update_ref.shape[2]
    for k in range(local):
        part = slice(k * dates, (k + 1) * dates)
        both = dot(rhs[part], by_ref[k], NT)
        update_ref[k] = both[:, :width]
        rows_ref[part, :] = left3(both[:, width:])


def reduce_kernel(both_ref, parent_ref, out_ref):
    half, dates, width = out_ref.shape
    first = lax.axis_index("core") * half
    for p in range(half):
        acc = None
        for k in range(both_ref.shape[0]):
            term = jnp.where(parent_ref[k : k + 1, :] == first + p, both_ref[k], 0.0)
            acc = term if acc is None else acc + term
        out_ref[p] = acc


def middle_kernel(got_ref, rhs_ref, inv_ref, out_ref, *, pieces):
    chips = got_ref.shape[0] // pieces
    tops, dates, width = rhs_ref.shape
    half = tops * pieces * chips // (tops * dates)
    span = dates // pieces
    piece = lax.axis_index("chip") ^ far_index(chips)
    p = lax.axis_index("core") * half + piece // span
    sums = [
        jnp.sum(got_ref[pl.ds(k, chips, stride=pieces), :], axis=0, keepdims=True)
        for k in range(pieces)
    ]
    left = rhs_ref[p, pl.ds((piece % span) * pieces, pieces), :] - jnp.concatenate(sums, axis=0)
    left = jnp.concatenate([left, jnp.zeros((8 - pieces % 8, width), F32)], axis=0)
    inv = inv_ref[p]
    sol = dot(left3(dot(left3(left), lanes3(inv), NT)), rows3(inv), NN)
    for k in range(pieces):
        out_ref[pl.ds(k, chips, stride=pieces), :] = jnp.broadcast_to(
            sol[k : k + 1, :], (chips, width)
        )


def last_kernel(parent_ref, top_ref, rows_ref, by_ref, out_hbm, top_hbm, out_ref, sems):
    local, dates, _ = out_ref.shape
    tops = top_ref.shape[0]
    copy_top = pltpu.make_async_copy(top_ref, top_hbm, sems.at[0])
    copy_top.start()
    first = lax.axis_index("core") * local
    copies = []
    for k in range(local):
        parent = parent_ref[pl.ds(first + k, 1), :]
        x = jnp.where(parent == 0, top_ref[0], 0.0)
        for p in range(1, tops):
            x = jnp.where(parent == p, top_ref[p], x)
        rows = rows_ref[k * dates : (k + 1) * dates, :]
        out_ref[k] = dot(jnp.concatenate([rows, left3(x)], axis=1), by_ref[k], NN)
        copies.append(pltpu.make_async_copy(out_ref.at[k], out_hbm.at[k], sems.at[1 + k]))
        copies[-1].start()
    copy_top.wait()
    for copy in copies:
        copy.wait()


VM = pl.BlockSpec(memory_space=pltpu.VMEM)
ANY = pl.BlockSpec(memory_space=pl.ANY)


def arr(*shape):
    return pltpu.VMEM(shape, F32)


def vmem(*arrays):
    return [pltpu.with_memory_space_constraint(a, pltpu.VMEM) for a in arrays]


def body(
    obs_coef, obs_data, obs_target, leaf_map, leaf_parent, leaf_inv, leaf_off, top_inv, top_rhs
):
    chips = lax.axis_size("chip")
    cores = lax.axis_size("core")
    planes = lax.axis_size("rhs")
    local = leaf_inv.shape[0]
    width = leaf_inv.shape[1]
    tops = top_inv.shape[0]
    dates, rows = obs_data.shape
    shard = obs_coef.shape[0]
    total = leaf_map.shape[0]
    slots = cores * CAP
    n_slots = chips * slots
    half = tops // cores
    pieces = half * dates // chips
    height = dates + shard + 8
    far = far_index(chips)

    payload, parent, forward_by, back_by = pl.pallas_call(
        lambda *refs: join_kernel(*refs, cores=cores),
        out_shape=(
            arr(height, rows),
            pltpu.VMEM((cores * local, LANES), I32),
            pltpu.VMEM((local, 2 * width, 3 * width), BF16),
            pltpu.VMEM((local, 6 * width, width), BF16),
        ),
        in_specs=[ANY] * 7,
        out_specs=(VM, VM, VM, VM),
        scratch_shapes=[
            pltpu.VMEM((1, total), I32),
            pltpu.VMEM((1, total), I32),
            pltpu.VMEM((1, rows), I32),
            pltpu.VMEM((local, width, width), F32),
            pltpu.VMEM((local, width, width), F32),
            pltpu.SemaphoreType.DMA((7,)),
        ],
        name="join",
    )(
        leaf_map.reshape(1, total),
        leaf_parent.reshape(1, total),
        obs_target.reshape(1, rows),
        obs_data,
        obs_coef,
        leaf_inv,
        leaf_off,
    )
    pair = lax.all_gather(payload, "core", axis=0)
    placed = pl.pallas_call(
        lambda *refs: pack_kernel(*refs, code_row=dates + shard + 1),
        out_shape=arr(n_slots, LANES),
        in_specs=[VM],
        out_specs=VM,
        name="pack",
    )(*vmem(pair))
    recv = exchange(placed.reshape(chips, slots, LANES), "chip", far)

    turned, share = pl.pallas_call(
        lambda *refs: turn_kernel(*refs, dates=dates),
        out_shape=(arr(LANES, n_slots), arr(planes, shard, n_slots)),
        in_specs=[VM],
        out_specs=(VM, VM),
        name="turn",
    )(*vmem(recv.reshape(n_slots, LANES)))
    coef = exchange(share, "rhs", planes // 2)
    parts, update = pl.pallas_call(
        lambda *refs: forward_kernel(*refs, shard=shard),
        out_shape=(pltpu.VMEM((local * dates, 3 * width), BF16), arr(local, dates, width)),
        in_specs=[VM, VM, VM],
        out_specs=(VM, VM),
        name="forward",
    )(*vmem(turned, coef, forward_by))
    both = lax.all_gather(update, "core", axis=0, tiled=True)
    contrib = pl.pallas_call(
        reduce_kernel,
        out_shape=arr(half, dates, width),
        in_specs=[VM, VM],
        out_specs=VM,
        name="reduce",
    )(*vmem(both, parent))
    got = exchange(contrib.reshape(chips, 1, pieces * width), "chip", far)
    out = pl.pallas_call(
        lambda *refs: middle_kernel(*refs, pieces=pieces),
        out_shape=arr(chips * pieces, width),
        in_specs=[VM, VM, VM],
        out_specs=VM,
        name="middle",
    )(*vmem(got.reshape(chips * pieces, width), top_rhs, top_inv))
    full = exchange(out.reshape(chips, 1, pieces * width), "chip", far)
    full = lax.all_gather(full.reshape(half, dates, width), "core", axis=0, tiled=True)
    return pl.pallas_call(
        last_kernel,
        out_shape=(
            jax.ShapeDtypeStruct((local, dates, width), F32),
            jax.ShapeDtypeStruct((tops, dates, width), F32),
        ),
        in_specs=[VM, VM, VM, VM],
        out_specs=(ANY, ANY),
        scratch_shapes=[
            pltpu.VMEM((local, dates, width), F32),
            pltpu.SemaphoreType.DMA((1 + local,)),
        ],
        name="last",
    )(*vmem(parent, full, parts, back_by))


def solution(mesh):
    devices = mesh.devices
    split = Mesh(devices.reshape(devices.shape[0] // 2, 2, -1), ("chip", "core", "rhs"))
    leaf = ("chip", "core")
    return jax.shard_map(
        body,
        mesh=split,
        in_specs=(
            P("rhs", leaf),
            P("rhs", leaf),
            P(leaf),
            P(),
            P(),
            P(leaf, None, None),
            P(leaf, None, None),
            P(),
            P(None, "rhs", None),
        ),
        out_specs=(P(leaf, "rhs", None), P(None, "rhs", None)),
        check_vma=False,
    )
```
